512 devices in a mesh: ctx: 128 (over x, z, y_lo), chan: 4 (over y_hi, core).
Axes of the slice: x: 4, y: 8 (y_hi: 2, y_lo: 4; y = y_hi * 4 + y_lo), z: 8, core: 2. Of those that a mesh axis runs over, the one named last changes fastest.
Arguments:
- signal: bfloat16 [128, 131072], P('chan', 'ctx'), may hold values from -6 to 6
- gating: bfloat16 [128, 131072], P('chan', 'ctx'), may hold values from -6 to 6
- cotangent: bfloat16 [128, 131072], P('chan', 'ctx'), may hold values from -6 to 6
- filters: float32 [32, 131072], P(None, 'ctx'), may hold values from -1 to 1
- skip_weight: float32 [128], P('chan'), may hold values from 0.5 to 1.5
Outputs:
- grad_signal: bfloat16 [128, 131072], P('chan', 'ctx')
- grad_gating: bfloat16 [128, 131072], P('chan', 'ctx')
- grad_filters: float32 [32, 131072], P('chan', 'ctx')
The draws below stay inside these ranges and needn't reach their ends.
All inputs are finite; a program needn't handle non-finite values.
Results may differ from the reference program's by a relative error of at most 0.0075.
Values may be sent and summed in bfloat16 or wider, within the bound.
A program may use at most 64 MiB of HBM per device.

```python
import math
import jax
import jax.numpy as jnp
from jax import lax

C = 128
FILT = 32
SEQ = 131072


def draw_filters(key, part):
    key_taps, key_reach = jax.random.split(jax.random.fold_in(key, 7))
    positions = jnp.arange(SEQ, dtype=jnp.float32)[None, :]
    lengths = jnp.exp(jax.random.uniform(key_reach, (FILT, 1), minval=math.log(40.0), maxval=math.log(4.0 * SEQ)))
    tap_values = jnp.clip(jax.random.normal(key_taps, (FILT, SEQ)), -4.0, 4.0)
    scaling = 1.0 / jnp.sqrt(jnp.minimum(lengths / 2.0, float(SEQ)))
    return (tap_values * jnp.exp(-positions / lengths) * scaling).astype(jnp.float32)


def block_scale(rng, extent, pieces, least, top_value):
    level, own = 1.0, jax.random.fold_in(rng, 6)
    for axis_at, blocks in pieces:
        draws = jnp.exp(jax.random.uniform(jax.random.fold_in(own, axis_at), (blocks,), jnp.float32, least / len(pieces), top_value / len(pieces)))
        level = level * jnp.repeat(draws, extent[axis_at] // blocks).reshape([-1 if axis == axis_at else 1 for axis in range(len(extent))])
    return level


def bell_draw(key, shape, width, reach, shards=(), held_as=jnp.bfloat16):
    values = width * jax.random.normal(key, shape, jnp.float32)
    if shards:
        values = values * block_scale(key, shape, shards, -0.22, 0.18)
    return jnp.clip(values, -reach, reach).astype(held_as)


def setup_inputs(seed: int = 0) -> dict:
    key_list = jax.random.split(jax.random.key(seed), 6)
    return {
        "signal": bell_draw(key_list[0], (C, SEQ), 1.0, 6.0, ((0, 4), (1, 128))),
        "gating": bell_draw(key_list[1], (C, SEQ), 1.0, 6.0, ((0, 4), (1, 128))),
        "cotangent": bell_draw(key_list[2], (C, SEQ), 1.0, 6.0, ((0, 4), (1, 128))),
        "filters": draw_filters(jax.random.fold_in(key_list[5], 71), 0),
        "skip_weight": jnp.clip(0.5 + 1.0 * jax.random.uniform(key_list[4], (C,), jnp.float32) ** block_scale(key_list[4], (C,), ((0, 4),), -0.2, 0.2), 0.5, 1.5),
    }


def reference(signal, gating, cotangent, filters, skip_weight):
    group_size = C // FILT
    padded = 2 * SEQ
    normal_scale = 1.0 / math.sqrt(SEQ * group_size)
    gated_grad = (cotangent.astype(jnp.float32) * gating.astype(jnp.float32)).astype(jnp.bfloat16)

    def regroup(array):
        return jnp.transpose(array.reshape(group_size, FILT, SEQ), (1, 0, 2))

    def ungroup(array):
        return jnp.transpose(array, (1, 0, 2)).reshape(C, SEQ)

    def one_filter(items):
        signal_rows, gated_rows, cot_rows, tap_row, weights = items
        signal_float = signal_rows.astype(jnp.float32)
        gated_float = gated_rows.astype(jnp.float32)
        signal_spec = jnp.fft.rfft(signal_float, n=padded, axis=-1)
        gated_spec = jnp.fft.rfft(gated_float, n=padded, axis=-1)
        tap_spec = jnp.fft.rfft(tap_row, n=padded)
        conv_out = jnp.fft.irfft(signal_spec * tap_spec[None, :], n=padded, axis=-1)[:, :SEQ]
        outputs = conv_out + weights[:, None] * signal_float
        grad_gating = (cot_rows.astype(jnp.float32) * outputs).astype(jnp.bfloat16)
        back_conv = jnp.fft.irfft(jnp.conj(tap_spec)[None, :] * gated_spec, n=padded, axis=-1)[:, :SEQ]
        grad_signal = (back_conv + weights[:, None] * gated_float).astype(jnp.bfloat16)
        correlation = jnp.fft.irfft(jnp.conj(signal_spec) * gated_spec, n=padded, axis=-1)[:, :SEQ]
        grad_row = (lax.optimization_barrier(jnp.sum(correlation, axis=0)) * normal_scale).astype(jnp.float32)
        return (grad_signal, grad_gating, grad_row)
    per_signal, per_gating, grad_filters = lax.map(one_filter, (regroup(signal), regroup(gated_grad), regroup(cotangent), filters, jnp.transpose(skip_weight.reshape(group_size, FILT))))
    return (ungroup(per_signal), ungroup(per_gating), grad_filters)
```

```python
import math

import jax
import jax.numpy as jnp
import numpy as np
from jax import lax
from jax.experimental import pallas as pl
from jax.experimental.pallas import tpu as pltpu
from jax.sharding import PartitionSpec as P

MESH = pl.DeviceIdType.MESH
F32 = jnp.float32
BF16 = jnp.bfloat16
COARSE = 512
FINE = 256
TILE = 256


def tables(total):
    shift = 0.25
    coarse = np.arange(COARSE) - shift
    angle = 2.0 * np.pi * ((coarse[:, None] * coarse[None, :]) / COARSE)
    big = np.concatenate([np.cos(angle), -np.sin(angle)], axis=1)
    fine = np.arange(FINE)
    angle = 2.0 * np.pi * ((coarse[:, None] * fine[None, :]) / total + coarse[:, None] * shift / COARSE)
    turn = np.concatenate([np.cos(angle), -np.sin(angle)], axis=1)
    angle = 2.0 * np.pi * ((fine[:, None] * fine[None, :]) % FINE) / FINE
    cosine, sine = np.cos(angle), np.sin(angle)
    ahead = np.block([[cosine, -sine], [sine, cosine]])
    back = np.block([[cosine, sine], [-sine, cosine]])
    as_bf16 = lambda table: jnp.asarray(table.astype(np.float32)).astype(BF16)
    return (as_bf16(big), jnp.asarray(turn.astype(np.float32)), as_bf16(ahead), as_bf16(back))


def dot(left, right):
    return jnp.dot(left, right, preferred_element_type=F32)


def kernel(
    signal, gating, cotangent, filters, big_hbm, turn_hbm, ahead_hbm, back_hbm,
    conv_out, back_out, corr_out,
    send, got, stage, big, turn, ahead, back, block, spec, mixed, leave, conv_in, back_in, corr_in,
    table_sem, own_sem, send_sem, got_sem, leave_sem, land_sem,
):
    place = lax.axis_index("ctx")
    chan = lax.axis_index("chan")
    rows = 32
    peers = 128
    lane = 128
    total = COARSE * FINE
    worker_low = 1 + chan % 2
    column = place // 4
    is_worker = place % 4 == worker_low
    home = column // 8
    foreign = home != chan

    table_copies = [
        pltpu.make_async_copy(big_hbm, big, table_sem.at[0]),
        pltpu.make_async_copy(turn_hbm, turn, table_sem.at[1]),
        pltpu.make_async_copy(ahead_hbm, ahead, table_sem.at[2]),
        pltpu.make_async_copy(back_hbm, back, table_sem.at[3]),
    ]

    barrier = pltpu.get_barrier_semaphore()

    def greet(ctx, other):
        pl.semaphore_signal(barrier, inc=1, device_id=(ctx, other), device_id_type=MESH)

    @pl.when(is_worker)
    def _():
        for copy in table_copies:
            copy.start()

        @pl.loop(1, peers)
        def _(step):
            greet((place + step) % peers, chan)

    @pl.loop(0, 8)
    def _(step):
        filt = 8 * chan + step
        for hop in range(1, 4):
            other = (chan + hop) % 4
            greet(4 * filt + 1 + other % 2, other)

    def spread(values, kind):
        for piece in range(8):
            stage[pl.ds(piece, rows, stride=8), :] = values[:, piece * lane : (piece + 1) * lane]
        send[:, kind] = stage[0 : rows * 8, :].reshape(rows, 8, lane).astype(BF16)

    spread(signal[...].astype(F32), 0)
    spread(filters[...], 1)
    gated = (cotangent[...].astype(F32) * gating[...].astype(F32)).astype(BF16)
    spread(gated.astype(F32), 2)

    @pl.when(is_worker)
    def _():
        @pl.when(foreign)
        def _():
            pl.semaphore_wait(barrier, 31 + peers)

        @pl.when(jnp.logical_not(foreign))
        def _():
            pl.semaphore_wait(barrier, 31)

    @pl.when(jnp.logical_not(is_worker))
    def _():
        pl.semaphore_wait(barrier, 32)

    parts = ((0, 2), (2, 3))
    for index, (low, high) in enumerate(parts):

        @pl.loop(0, rows)
        def _(step):
            filt = (column + step) % rows
            target = 4 * filt + worker_low

            @pl.when(target != place)
            def _():
                pltpu.make_async_remote_copy(
                    send.at[filt, low:high], got.at[place, low:high],
                    send_sem.at[index], got_sem.at[index],
                    device_id=(target, chan), device_id_type=MESH,
                ).start()

    def drain(ref, sem):
        pltpu.make_async_copy(ref, ref, sem).wait()

    def ahead_transform(kind):
        stage[...] = got[:, kind].astype(F32).reshape(peers * 8, lane)
        for half in range(2):
            block[:, half * lane : (half + 1) * lane] = stage[pl.ds(half, COARSE, stride=2), :].astype(BF16)

        @pl.loop(0, COARSE // TILE)
        def _(step):
            at = pl.ds(pl.multiple_of(step * TILE, TILE), TILE)
            real = dot(big[at, 0:COARSE], block[...])
            imag = dot(big[at, COARSE:], block[...])
            cosine = turn[at, 0:FINE]
            sine = turn[at, FINE:]
            turned = jnp.concatenate(
                [real * cosine - imag * sine, real * sine + imag * cosine], axis=1
            ).astype(BF16)
            spec[kind, at, :] = dot(turned, ahead[...])

    def back_transform(left, right, conjugate, kind):
        @pl.loop(0, COARSE // TILE)
        def _(step):
            at = pl.ds(pl.multiple_of(step * TILE, TILE), TILE)
            left_real = spec[left, at, 0:FINE]
            left_imag = spec[left, at, FINE:]
            right_real = spec[right, at, 0:FINE]
            right_imag = spec[right, at, FINE:]
            if conjugate:
                real = left_real * right_real + left_imag * right_imag
                imag = left_real * right_imag - left_imag * right_real
            else:
                real = left_real * right_real - left_imag * right_imag
                imag = left_real * right_imag + left_imag * right_real
            joined = jnp.concatenate([real, imag], axis=1).astype(BF16)
            half = dot(joined, back[...])
            real, imag = half[:, 0:FINE], half[:, FINE:]
            cosine = turn[at, 0:FINE]
            sine = turn[at, FINE:]
            mixed[at, :] = (real * cosine + imag * sine).astype(BF16)
            low = pl.ds(pl.multiple_of(COARSE + step * TILE, TILE), TILE)
            mixed[low, :] = (imag * cosine - real * sine).astype(BF16)

        @pl.loop(0, COARSE // TILE)
        def _(step):
            at = pl.ds(pl.multiple_of(step * TILE, TILE), TILE)
            time = dot(big[at, :], mixed[...]) * (1.0 / total)
            for part in range(2):
                stage[pl.ds(2 * step * TILE + part, TILE, stride=2), :] = time[
                    :, part * lane : (part + 1) * lane
                ]

        leave[kind] = stage[...].reshape(peers, 8, lane).astype(BF16)

    def scatter(kind, landing):
        @pl.loop(1, peers)
        def _(step):
            target = (place + step) % peers
            pltpu.make_async_remote_copy(
                leave.at[kind, target], landing.at[column],
                leave_sem.at[kind], land_sem.at[kind],
                device_id=(target, chan), device_id_type=MESH,
            ).start()

        pltpu.make_async_copy(leave.at[kind, place], landing.at[column], own_sem.at[1 + kind]).start()

    @pl.when(is_worker)
    def _():
        pltpu.make_async_copy(send.at[column], got.at[place], own_sem.at[0]).start()
        for copy in table_copies:
            copy.wait()
        pltpu.make_async_copy(send.at[column], got.at[place], own_sem.at[0]).wait()
        drain(got.at[0 : peers - 1, 0:2], got_sem.at[0])
        ahead_transform(0)
        ahead_transform(1)
        back_transform(0, 1, False, 0)
        scatter(0, conv_in)
        drain(got.at[0 : peers - 1, 2:3], got_sem.at[1])
        ahead_transform(2)
        back_transform(1, 2, True, 1)
        scatter(1, back_in)
        back_transform(0, 2, True, 2)

        @pl.loop(0, peers)
        def _(step):
            target = (place + step) % peers

            @pl.when(jnp.logical_or(foreign, step > 0))
            def _():
                pltpu.make_async_remote_copy(
                    leave.at[2, target], corr_in.at[column % 8, chan],
                    leave_sem.at[2], land_sem.at[2],
                    device_id=(target, home), device_id_type=MESH,
                ).start()

        @pl.when(jnp.logical_not(foreign))
        def _():
            pltpu.make_async_copy(leave.at[2, place], corr_in.at[column % 8, chan], own_sem.at[3]).start()

        drain(send.at[0 : rows - 1, 0:2], send_sem.at[0])
        drain(send.at[0 : rows - 1, 2:3], send_sem.at[1])
        for kind, landing in ((0, conv_in), (1, back_in)):
            pltpu.make_async_copy(leave.at[kind, place], landing.at[column], own_sem.at[1 + kind]).wait()
            drain(landing.at[0 : rows - 1], land_sem.at[kind])

        @pl.when(foreign)
        def _():
            drain(corr_in, land_sem.at[2])

        @pl.when(jnp.logical_not(foreign))
        def _():
            pltpu.make_async_copy(leave.at[2, place], corr_in.at[column % 8, chan], own_sem.at[3]).wait()
            drain(leave.at[2, 0 : rows - 1], land_sem.at[2])

    @pl.when(jnp.logical_not(is_worker))
    def _():
        drain(send.at[0:rows, 0:2], send_sem.at[0])
        drain(send.at[0:rows, 2:3], send_sem.at[1])
        drain(conv_in, land_sem.at[0])
        drain(back_in, land_sem.at[1])
        drain(corr_in, land_sem.at[2])

    def gather(values, count, result):
        stage[0 : count * 8, :] = values.reshape(count * 8, lane)
        for piece in range(8):
            result[:, piece * lane : (piece + 1) * lane] = stage[pl.ds(piece, count, stride=8), :].astype(
                result.dtype
            )

    gather(conv_in[...].astype(F32), rows, conv_out)
    gather(back_in[...].astype(F32), rows, back_out)
    gather(jnp.sum(corr_in[...].astype(F32), axis=1), 8, corr_out)

    @pl.when(is_worker)
    def _():
        drain(leave.at[0, 0 : peers - 1], leave_sem.at[0])
        drain(leave.at[1, 0 : peers - 1], leave_sem.at[1])

        @pl.when(foreign)
        def _():
            drain(leave.at[2], leave_sem.at[2])

        @pl.when(jnp.logical_not(foreign))
        def _():
            drain(leave.at[2, 0 : peers - 1], leave_sem.at[2])


def exchange(signal, gating, cotangent, filters):
    rows, length = signal.shape
    total = COARSE * FINE
    peers = total // length
    table_list = tables(total)
    vmem = pl.BlockSpec(memory_space=pltpu.VMEM)
    hbm = pl.BlockSpec(memory_space=pl.ANY)
    return pl.pallas_call(
        kernel,
        out_shape=(
            jax.ShapeDtypeStruct((rows, length), F32),
            jax.ShapeDtypeStruct((rows, length), F32),
            jax.ShapeDtypeStruct((8, length), F32),
        ),
        in_specs=[vmem] * 4 + [hbm] * 4,
        out_specs=(vmem, vmem, vmem),
        scratch_shapes=[
            pltpu.VMEM((rows, 3, 8, 128), BF16),
            pltpu.VMEM((peers, 3, 8, 128), BF16),
            pltpu.VMEM((peers * 8, 128), F32),
            pltpu.VMEM((COARSE, 2 * COARSE), BF16),
            pltpu.VMEM((COARSE, 2 * FINE), F32),
            pltpu.VMEM((2 * FINE, 2 * FINE), BF16),
            pltpu.VMEM((2 * FINE, 2 * FINE), BF16),
            pltpu.VMEM((COARSE, FINE), BF16),
            pltpu.VMEM((3, COARSE, 2 * FINE), F32),
            pltpu.VMEM((2 * COARSE, FINE), BF16),
            pltpu.VMEM((3, peers, 8, 128), BF16),
            pltpu.VMEM((rows, 8, 128), BF16),
            pltpu.VMEM((rows, 8, 128), BF16),
            pltpu.VMEM((8, 4, 8, 128), BF16),
            pltpu.SemaphoreType.DMA((4,)),
            pltpu.SemaphoreType.DMA((4,)),
            pltpu.SemaphoreType.DMA((2,)),
            pltpu.SemaphoreType.DMA((2,)),
            pltpu.SemaphoreType.DMA((3,)),
            pltpu.SemaphoreType.DMA((3,)),
        ],
        compiler_params=pltpu.CompilerParams(
            collective_id=0, has_side_effects=True, vmem_limit_bytes=40 * 1024 * 1024
        ),
        name="exchange",
    )(signal, gating, cotangent, filters, *table_list)


def per_device(signal, gating, cotangent, filters, skip_weight):
    rows, length = signal.shape
    conv, back, corr = exchange(signal, gating, cotangent, filters)
    weight = skip_weight[:, None]
    cot = cotangent.astype(F32)
    gated = (cot * gating.astype(F32)).astype(BF16).astype(F32)
    grad_gating = (cot * (conv + weight * signal.astype(F32))).astype(BF16)
    grad_signal = (back + weight * gated).astype(BF16)
    group = lax.axis_size("chan") * rows // filters.shape[0]
    grad_filters = corr * (1.0 / math.sqrt(COARSE * FINE * group))
    return (grad_signal, grad_gating, grad_filters)


def solution(mesh):
    in_specs = (P("chan", "ctx"), P("chan", "ctx"), P("chan", "ctx"), P(None, "ctx"), P("chan"))
    out_specs = (P("chan", "ctx"), P("chan", "ctx"), P("chan", "ctx"))
    return jax.shard_map(
        per_device, mesh=mesh, in_specs=in_specs, out_specs=out_specs, check_vma=False
    )
```

```python
import math

import jax
import jax.numpy as jnp
import numpy as np
from jax import lax
from jax.experimental import pallas as pl
from jax.experimental.pallas import tpu as pltpu
from jax.sharding import PartitionSpec as P

MESH = pl.DeviceIdType.MESH
F32 = jnp.float32
BF16 = jnp.bfloat16
COARSE = 512
FINE = 256
TILE = 256


def tables(total):
    shift = 0.25
    coarse = np.arange(COARSE) - shift
    angle = 2.0 * np.pi * ((coarse[:, None] * coarse[None, :]) / COARSE)
    big = np.concatenate([np.cos(angle), -np.sin(angle)], axis=1)
    fine = np.arange(FINE)
    angle = 2.0 * np.pi * ((coarse[:, None] * fine[None, :]) / total + coarse[:, None] * shift / COARSE)
    turn = np.concatenate([np.cos(angle), -np.sin(angle)], axis=1)
    angle = 2.0 * np.pi * ((fine[:, None] * fine[None, :]) % FINE) / FINE
    cosine, sine = np.cos(angle), np.sin(angle)
    ahead = np.block([[cosine, -sine], [sine, cosine]])
    back = np.block([[cosine, sine], [-sine, cosine]])
    as_bf16 = lambda table: jnp.asarray(table.astype(np.float32)).astype(BF16)
    return (as_bf16(big), jnp.asarray(turn.astype(np.float32)), as_bf16(ahead), as_bf16(back))


def dot(left, right):
    return jnp.dot(left, right, preferred_element_type=F32)


def kernel(
    signal_hbm, gating_hbm, cotangent_hbm, filters_hbm, weight_hbm, big_hbm, turn_hbm, ahead_hbm, back_hbm,
    conv_out, back_out, corr_out,
    signal, gating, cotangent, filters, weight, direct_signal, direct_gated, send, got, stage, big, turn, ahead, back, block, spec, mixed, leave, conv_in, back_in, corr_in,
    load_sem, table_sem, own_sem, send_sem, got_sem, leave_sem, land_sem,
):
    place = lax.axis_index("ctx")
    chan = lax.axis_index("chan")
    rows = 32
    peers = 128
    lane = 128
    total = COARSE * FINE
    worker_low = 1 + chan % 2
    column = place // 4
    is_worker = place % 4 == worker_low
    home = column // 8
    foreign = home != chan

    load_copies = [
        pltpu.make_async_copy(source, target, load_sem.at[index])
        for index, (source, target) in enumerate(
            (
                (signal_hbm, signal),
                (filters_hbm, filters),
                (cotangent_hbm, cotangent),
                (gating_hbm, gating),
                (weight_hbm, weight),
            )
        )
    ]
    for copy in load_copies:
        copy.start()
    table_copies = [
        pltpu.make_async_copy(big_hbm, big, table_sem.at[0]),
        pltpu.make_async_copy(turn_hbm, turn, table_sem.at[1]),
        pltpu.make_async_copy(ahead_hbm, ahead, table_sem.at[2]),
        pltpu.make_async_copy(back_hbm, back, table_sem.at[3]),
    ]

    barrier = pltpu.get_barrier_semaphore()

    def greet(ctx, other):
        pl.semaphore_signal(barrier, inc=1, device_id=(ctx, other), device_id_type=MESH)

    @pl.when(is_worker)
    def _():
        for copy in table_copies:
            copy.start()

        @pl.loop(1, peers)
        def _(step):
            greet((place + step) % peers, chan)

    @pl.loop(0, 8)
    def _(step):
        filt = 8 * chan + step
        for hop in range(1, 4):
            other = (chan + hop) % 4
            greet(4 * filt + 1 + other % 2, other)

    def spread(values, kind):
        for piece in range(8):
            stage[pl.ds(piece, rows, stride=8), :] = values[:, piece * lane : (piece + 1) * lane]
        send[:, kind] = stage[0 : rows * 8, :].reshape(rows, 8, lane).astype(BF16)

    load_copies[0].wait()
    spread(signal[...].astype(F32), 0)
    load_copies[1].wait()
    spread(filters[...], 1)
    load_copies[2].wait()
    load_copies[3].wait()
    gated = (cotangent[...].astype(F32) * gating[...].astype(F32)).astype(BF16)
    spread(gated.astype(F32), 2)
    load_copies[4].wait()
    across = weight[...].reshape(1, rows) * jnp.ones((rows, 1), F32)
    diagonal = lax.broadcasted_iota(jnp.int32, (rows, rows), 0) == lax.broadcasted_iota(
        jnp.int32, (rows, rows), 1
    )
    down = jnp.sum(jnp.where(diagonal, across, 0.0), axis=1, keepdims=True)
    direct_signal[...] = down * signal[...].astype(F32)
    direct_gated[...] = down * gated.astype(F32)

    @pl.when(is_worker)
    def _():
        @pl.when(foreign)
        def _():
            pl.semaphore_wait(barrier, 31 + peers)

        @pl.when(jnp.logical_not(foreign))
        def _():
            pl.semaphore_wait(barrier, 31)

    @pl.when(jnp.logical_not(is_worker))
    def _():
        pl.semaphore_wait(barrier, 32)

    parts = ((0, 2), (2, 3))
    for index, (low, high) in enumerate(parts):

        @pl.loop(0, rows)
        def _(step):
            filt = (column + step) % rows
            target = 4 * filt + worker_low

            @pl.when(target != place)
            def _():
                pltpu.make_async_remote_copy(
                    send.at[filt, low:high], got.at[place, low:high],
                    send_sem.at[index], got_sem.at[index],
                    device_id=(target, chan), device_id_type=MESH,
                ).start()

    def drain(ref, sem):
        pltpu.make_async_copy(ref, ref, sem).wait()

    def ahead_transform(kind):
        stage[...] = got[:, kind].astype(F32).reshape(peers * 8, lane)
        for half in range(2):
            block[:, half * lane : (half + 1) * lane] = stage[pl.ds(half, COARSE, stride=2), :].astype(BF16)

        for step in range(COARSE // TILE):
            at = pl.ds(step * TILE, TILE)
            real = dot(big[at, 0:COARSE], block[...])
            imag = dot(big[at, COARSE:], block[...])
            cosine = turn[at, 0:FINE]
            sine = turn[at, FINE:]
            turned = jnp.concatenate(
                [real * cosine - imag * sine, real * sine + imag * cosine], axis=1
            ).astype(BF16)
            spec[kind, at, :] = dot(turned, ahead[...])

    def back_transform(left, right, conjugate, kind):
        for step in range(COARSE // TILE):
            at = pl.ds(step * TILE, TILE)
            left_real = spec[left, at, 0:FINE]
            left_imag = spec[left, at, FINE:]
            right_real = spec[right, at, 0:FINE]
            right_imag = spec[right, at, FINE:]
            if conjugate:
                real = left_real * right_real + left_imag * right_imag
                imag = left_real * right_imag - left_imag * right_real
            else:
                real = left_real * right_real - left_imag * right_imag
                imag = left_real * right_imag + left_imag * right_real
            joined = jnp.concatenate([real, imag], axis=1).astype(BF16)
            half = dot(joined, back[...])
            real, imag = half[:, 0:FINE], half[:, FINE:]
            cosine = turn[at, 0:FINE]
            sine = turn[at, FINE:]
            mixed[at, :] = (real * cosine + imag * sine).astype(BF16)
            low = pl.ds(COARSE + step * TILE, TILE)
            mixed[low, :] = (imag * cosine - real * sine).astype(BF16)

        for step in range(COARSE // TILE):
            at = pl.ds(step * TILE, TILE)
            time = dot(big[at, :], mixed[...]) * (1.0 / total)
            for part in range(2):
                stage[pl.ds(2 * step * TILE + part, TILE, stride=2), :] = time[
                    :, part * lane : (part + 1) * lane
                ]

        leave[kind] = stage[...].reshape(peers, 8, lane).astype(BF16)

    def scatter(kind, landing):
        @pl.loop(1, peers)
        def _(step):
            target = (place + step) % peers
            pltpu.make_async_remote_copy(
                leave.at[kind, target], landing.at[column],
                leave_sem.at[kind], land_sem.at[kind],
                device_id=(target, chan), device_id_type=MESH,
            ).start()

        pltpu.make_async_copy(leave.at[kind, place], landing.at[column], own_sem.at[1 + kind]).start()

    @pl.when(is_worker)
    def _():
        pltpu.make_async_copy(send.at[column], got.at[place], own_sem.at[0]).start()
        for copy in table_copies:
            copy.wait()
        pltpu.make_async_copy(send.at[column], got.at[place], own_sem.at[0]).wait()
        drain(got.at[0 : peers - 1, 0:2], got_sem.at[0])
        ahead_transform(0)
        ahead_transform(1)
        back_transform(0, 1, False, 0)
        scatter(0, conv_in)
        drain(got.at[0 : peers - 1, 2:3], got_sem.at[1])
        ahead_transform(2)
        back_transform(1, 2, True, 1)
        scatter(1, back_in)
        back_transform(0, 2, True, 2)

        @pl.loop(0, peers)
        def _(step):
            target = (place + step) % peers

            @pl.when(jnp.logical_or(foreign, step > 0))
            def _():
                pltpu.make_async_remote_copy(
                    leave.at[2, target], corr_in.at[column % 8, chan],
                    leave_sem.at[2], land_sem.at[2],
                    device_id=(target, home), device_id_type=MESH,
                ).start()

        @pl.when(jnp.logical_not(foreign))
        def _():
            pltpu.make_async_copy(leave.at[2, place], corr_in.at[column % 8, chan], own_sem.at[3]).start()

        drain(send.at[0 : rows - 1, 0:2], send_sem.at[0])
        drain(send.at[0 : rows - 1, 2:3], send_sem.at[1])
        for kind, landing in ((0, conv_in), (1, back_in)):
            pltpu.make_async_copy(leave.at[kind, place], landing.at[column], own_sem.at[1 + kind]).wait()
            drain(landing.at[0 : rows - 1], land_sem.at[kind])

        @pl.when(foreign)
        def _():
            drain(corr_in, land_sem.at[2])

        @pl.when(jnp.logical_not(foreign))
        def _():
            pltpu.make_async_copy(leave.at[2, place], corr_in.at[column % 8, chan], own_sem.at[3]).wait()
            drain(leave.at[2, 0 : rows - 1], land_sem.at[2])

    @pl.when(jnp.logical_not(is_worker))
    def _():
        drain(send.at[0:rows, 0:2], send_sem.at[0])
        drain(send.at[0:rows, 2:3], send_sem.at[1])
        drain(conv_in, land_sem.at[0])
        drain(back_in, land_sem.at[1])
        drain(corr_in, land_sem.at[2])

    def gather(values, count, direct, factor, result):
        stage[0 : count * 8, :] = values.reshape(count * 8, lane)
        for piece in range(8):
            part = slice(piece * lane, (piece + 1) * lane)
            value = stage[pl.ds(piece, count, stride=8), :]
            if direct is not None:
                value = value + direct[:, part]
            result[:, part] = value if factor is None else value * factor[:, part].astype(F32)

    gather(conv_in[...].astype(F32), rows, direct_signal, cotangent, conv_out)
    gather(back_in[...].astype(F32), rows, direct_gated, None, back_out)
    gather(jnp.sum(corr_in[...].astype(F32), axis=1), 8, None, None, corr_out)

    @pl.when(is_worker)
    def _():
        drain(leave.at[0, 0 : peers - 1], leave_sem.at[0])
        drain(leave.at[1, 0 : peers - 1], leave_sem.at[1])

        @pl.when(foreign)
        def _():
            drain(leave.at[2], leave_sem.at[2])

        @pl.when(jnp.logical_not(foreign))
        def _():
            drain(leave.at[2, 0 : peers - 1], leave_sem.at[2])


def exchange(signal, gating, cotangent, filters, skip_weight):
    rows, length = signal.shape
    total = COARSE * FINE
    peers = total // length
    operands = (signal, gating, cotangent, filters, skip_weight, *tables(total))
    vmem = pl.BlockSpec(memory_space=pltpu.VMEM)
    hbm = pl.BlockSpec(memory_space=pltpu.HBM)
    return pl.pallas_call(
        kernel,
        out_shape=(
            jax.ShapeDtypeStruct((rows, length), F32),
            jax.ShapeDtypeStruct((rows, length), F32),
            jax.ShapeDtypeStruct((8, length), F32),
        ),
        in_specs=[hbm] * 9,
        out_specs=(vmem, vmem, vmem),
        scratch_shapes=[
            pltpu.VMEM((rows, length), BF16),
            pltpu.VMEM((rows, length), BF16),
            pltpu.VMEM((rows, length), BF16),
            pltpu.VMEM((rows, length), F32),
            pltpu.VMEM((rows,), F32),
            pltpu.VMEM((rows, length), F32),
            pltpu.VMEM((rows, length), F32),
            pltpu.VMEM((rows, 3, 8, 128), BF16),
            pltpu.VMEM((peers, 3, 8, 128), BF16),
            pltpu.VMEM((peers * 8, 128), F32),
            pltpu.VMEM((COARSE, 2 * COARSE), BF16),
            pltpu.VMEM((COARSE, 2 * FINE), F32),
            pltpu.VMEM((2 * FINE, 2 * FINE), BF16),
            pltpu.VMEM((2 * FINE, 2 * FINE), BF16),
            pltpu.VMEM((COARSE, FINE), BF16),
            pltpu.VMEM((3, COARSE, 2 * FINE), F32),
            pltpu.VMEM((2 * COARSE, FINE), BF16),
            pltpu.VMEM((3, peers, 8, 128), BF16),
            pltpu.VMEM((rows, 8, 128), BF16),
            pltpu.VMEM((rows, 8, 128), BF16),
            pltpu.VMEM((8, 4, 8, 128), BF16),
            pltpu.SemaphoreType.DMA((5,)),
            pltpu.SemaphoreType.DMA((4,)),
            pltpu.SemaphoreType.DMA((4,)),
            pltpu.SemaphoreType.DMA((2,)),
            pltpu.SemaphoreType.DMA((2,)),
            pltpu.SemaphoreType.DMA((3,)),
            pltpu.SemaphoreType.DMA((3,)),
        ],
        compiler_params=pltpu.CompilerParams(
            collective_id=0, has_side_effects=True, vmem_limit_bytes=40 * 1024 * 1024
        ),
        name="exchange",
    )(*[pltpu.with_memory_space_constraint(each, pltpu.HBM) for each in operands])


def per_device(signal, gating, cotangent, filters, skip_weight):
    rows = signal.shape[0]
    conv, back, corr = exchange(signal, gating, cotangent, filters, skip_weight)
    grad_gating = conv.astype(BF16)
    grad_signal = back.astype(BF16)
    group = lax.axis_size("chan") * rows // filters.shape[0]
    grad_filters = corr * (1.0 / math.sqrt(COARSE * FINE * group))
    return (grad_signal, grad_gating, grad_filters)


def solution(mesh):
    in_specs = (P("chan", "ctx"), P("chan", "ctx"), P("chan", "ctx"), P(None, "ctx"), P("chan"))
    out_specs = (P("chan", "ctx"), P("chan", "ctx"), P("chan", "ctx"))
    return jax.shard_map(
        per_device, mesh=mesh, in_specs=in_specs, out_specs=out_specs, check_vma=False
    )
```

```python
import math

import jax
import jax.numpy as jnp
import numpy as np
from jax import lax
from jax.experimental import pallas as pl
from jax.experimental.pallas import tpu as pltpu
from jax.sharding import PartitionSpec as P

MESH = pl.DeviceIdType.MESH
F32 = jnp.float32
BF16 = jnp.bfloat16
COARSE = 512
FINE = 256
TILE = 256


def tables(total):
    shift = 0.25
    coarse = np.arange(COARSE) - shift
    angle = 2.0 * np.pi * ((coarse[:, None] * coarse[None, :]) / COARSE)
    big = np.concatenate([np.cos(angle), -np.sin(angle)], axis=1)
    fine = np.arange(FINE)
    angle = 2.0 * np.pi * ((coarse[:, None] * fine[None, :]) / total + coarse[:, None] * shift / COARSE)
    turn = np.concatenate([np.cos(angle), -np.sin(angle)], axis=1)
    angle = 2.0 * np.pi * ((fine[:, None] * fine[None, :]) % FINE) / FINE
    cosine, sine = np.cos(angle), np.sin(angle)
    ahead = np.block([[cosine, -sine], [sine, cosine]])
    back = np.block([[cosine, sine], [-sine, cosine]])
    as_bf16 = lambda table: jnp.asarray(table.astype(np.float32)).astype(BF16)
    return (as_bf16(big), jnp.asarray(turn.astype(np.float32)), as_bf16(ahead), as_bf16(back))


def dot(left, right):
    return jnp.dot(left, right, preferred_element_type=F32)


def kernel(
    signal_hbm, gating_hbm, cotangent_hbm, filters_hbm, weight_hbm, big_hbm, turn_hbm, ahead_hbm, back_hbm,
    conv_in, back_in, corr_in, direct_signal, direct_gated, cotangent,
    signal, gating, filters, weight, send, got, stage, big, turn, ahead, back, block, spec, mixed, leave,
    load_sem, table_sem, own_sem, send_sem, got_sem, leave_sem, land_sem,
):
    place = lax.axis_index("ctx")
    chan = lax.axis_index("chan")
    rows = 32
    peers = 128
    lane = 128
    total = COARSE * FINE
    column = place // 4

    def worker_of(filt, channel):
        return 4 * filt + (1 + channel % 2 + 2 * ((filt + filt // 8) % 2)) % 4

    is_worker = place == worker_of(column, chan)
    home = column // 8
    foreign = home != chan

    load_copies = [
        pltpu.make_async_copy(source, target, load_sem.at[index])
        for index, (source, target) in enumerate(
            (
                (signal_hbm, signal),
                (filters_hbm, filters),
                (cotangent_hbm, cotangent),
                (gating_hbm, gating),
                (weight_hbm, weight),
            )
        )
    ]
    for copy in load_copies:
        copy.start()
    table_copies = [
        pltpu.make_async_copy(big_hbm, big, table_sem.at[0]),
        pltpu.make_async_copy(turn_hbm, turn, table_sem.at[1]),
        pltpu.make_async_copy(ahead_hbm, ahead, table_sem.at[2]),
        pltpu.make_async_copy(back_hbm, back, table_sem.at[3]),
    ]

    barrier = pltpu.get_barrier_semaphore()

    def greet(ctx, other):
        pl.semaphore_signal(barrier, inc=1, device_id=(ctx, other), device_id_type=MESH)

    @pl.when(is_worker)
    def _():
        for copy in table_copies:
            copy.start()

        @pl.loop(1, peers)
        def _(step):
            greet((place + step) % peers, chan)

    @pl.loop(0, 8)
    def _(step):
        filt = 8 * chan + step
        for hop in range(1, 4):
            other = (chan + hop) % 4
            greet(worker_of(filt, other), other)

    def spread(values, kind):
        for piece in range(8):
            stage[pl.ds(piece, rows, stride=8), :] = values[:, piece * lane : (piece + 1) * lane]
        send[:, kind] = stage[0 : rows * 8, :].reshape(rows, 8, lane).astype(BF16)

    load_copies[0].wait()
    spread(signal[...].astype(F32), 0)
    load_copies[1].wait()
    spread(filters[...], 1)
    load_copies[2].wait()
    load_copies[3].wait()
    gated = (cotangent[...].astype(F32) * gating[...].astype(F32)).astype(BF16)
    spread(gated.astype(F32), 2)
    load_copies[4].wait()
    across = weight[...].reshape(1, rows) * jnp.ones((rows, 1), F32)
    diagonal = lax.broadcasted_iota(jnp.int32, (rows, rows), 0) == lax.broadcasted_iota(
        jnp.int32, (rows, rows), 1
    )
    down = jnp.sum(jnp.where(diagonal, across, 0.0), axis=1, keepdims=True)
    direct_signal[...] = down * signal[...].astype(F32)
    direct_gated[...] = down * gated.astype(F32)

    @pl.when(is_worker)
    def _():
        @pl.when(foreign)
        def _():
            pl.semaphore_wait(barrier, 31 + peers)

        @pl.when(jnp.logical_not(foreign))
        def _():
            pl.semaphore_wait(barrier, 31)

    @pl.when(jnp.logical_not(is_worker))
    def _():
        pl.semaphore_wait(barrier, 32)

    parts = ((0, 2), (2, 3))
    for index, (low, high) in enumerate(parts):

        @pl.loop(0, rows)
        def _(step):
            filt = (column + step) % rows
            target = worker_of(filt, chan)

            @pl.when(target != place)
            def _():
                pltpu.make_async_remote_copy(
                    send.at[filt, low:high], got.at[place, low:high],
                    send_sem.at[index], got_sem.at[index],
                    device_id=(target, chan), device_id_type=MESH,
                ).start()

    def turn_to(step):
        return (place + step) % peers

    def drain(ref, sem):
        pltpu.make_async_copy(ref, ref, sem).wait()

    def ahead_transform(kind):
        stage[...] = got[:, kind].astype(F32).reshape(peers * 8, lane)
        for half in range(2):
            block[:, half * lane : (half + 1) * lane] = stage[pl.ds(half, COARSE, stride=2), :].astype(BF16)

        for step in range(COARSE // TILE):
            at = pl.ds(step * TILE, TILE)
            real = dot(big[at, 0:COARSE], block[...])
            imag = dot(big[at, COARSE:], block[...])
            cosine = turn[at, 0:FINE]
            sine = turn[at, FINE:]
            turned = jnp.concatenate(
                [real * cosine - imag * sine, real * sine + imag * cosine], axis=1
            ).astype(BF16)
            spec[kind, at, :] = dot(turned, ahead[...])

    def back_transform(left, right, conjugate, kind):
        for step in range(COARSE // TILE):
            at = pl.ds(step * TILE, TILE)
            left_real = spec[left, at, 0:FINE]
            left_imag = spec[left, at, FINE:]
            right_real = spec[right, at, 0:FINE]
            right_imag = spec[right, at, FINE:]
            if conjugate:
                real = left_real * right_real + left_imag * right_imag
                imag = left_real * right_imag - left_imag * right_real
            else:
                real = left_real * right_real - left_imag * right_imag
                imag = left_real * right_imag + left_imag * right_real
            joined = jnp.concatenate([real, imag], axis=1).astype(BF16)
            half = dot(joined, back[...])
            real, imag = half[:, 0:FINE], half[:, FINE:]
            cosine = turn[at, 0:FINE]
            sine = turn[at, FINE:]
            mixed[at, :] = (real * cosine + imag * sine).astype(BF16)
            low = pl.ds(COARSE + step * TILE, TILE)
            mixed[low, :] = (imag * cosine - real * sine).astype(BF16)

        for step in range(COARSE // TILE):
            at = pl.ds(step * TILE, TILE)
            time = dot(big[at, :], mixed[...]) * (1.0 / total)
            for part in range(2):
                stage[pl.ds(2 * step * TILE + part, TILE, stride=2), :] = time[
                    :, part * lane : (part + 1) * lane
                ]

        leave[kind] = stage[...].reshape(peers, 8, lane).astype(BF16)

    def scatter(kind, landing):
        @pl.loop(1, peers)
        def _(step):
            target = turn_to(step)
            pltpu.make_async_remote_copy(
                leave.at[kind, target], landing.at[column],
                leave_sem.at[kind], land_sem.at[kind],
                device_id=(target, chan), device_id_type=MESH,
            ).start()

        pltpu.make_async_copy(leave.at[kind, place], landing.at[column], own_sem.at[1 + kind]).start()

    @pl.when(is_worker)
    def _():
        pltpu.make_async_copy(send.at[column], got.at[place], own_sem.at[0]).start()
        for copy in table_copies:
            copy.wait()
        pltpu.make_async_copy(send.at[column], got.at[place], own_sem.at[0]).wait()
        drain(got.at[0 : peers - 1, 0:2], got_sem.at[0])
        ahead_transform(0)
        ahead_transform(1)
        back_transform(0, 1, False, 0)
        scatter(0, conv_in)
        drain(got.at[0 : peers - 1, 2:3], got_sem.at[1])
        ahead_transform(2)
        back_transform(0, 2, True, 2)

        @pl.loop(0, peers)
        def _(step):
            target = turn_to(step)

            @pl.when(jnp.logical_or(foreign, step > 0))
            def _():
                pltpu.make_async_remote_copy(
                    leave.at[2, target], corr_in.at[column % 8, chan],
                    leave_sem.at[2], land_sem.at[2],
                    device_id=(target, home), device_id_type=MESH,
                ).start()

        @pl.when(jnp.logical_not(foreign))
        def _():
            pltpu.make_async_copy(leave.at[2, place], corr_in.at[column % 8, chan], own_sem.at[3]).start()

        back_transform(1, 2, True, 1)
        scatter(1, back_in)

        drain(send.at[0 : rows - 1, 0:2], send_sem.at[0])
        drain(send.at[0 : rows - 1, 2:3], send_sem.at[1])
        for kind, landing in ((0, conv_in), (1, back_in)):
            pltpu.make_async_copy(leave.at[kind, place], landing.at[column], own_sem.at[1 + kind]).wait()
            drain(landing.at[0 : rows - 1], land_sem.at[kind])

        @pl.when(foreign)
        def _():
            drain(corr_in, land_sem.at[2])

        @pl.when(jnp.logical_not(foreign))
        def _():
            pltpu.make_async_copy(leave.at[2, place], corr_in.at[column % 8, chan], own_sem.at[3]).wait()
            drain(leave.at[2, 0 : rows - 1], land_sem.at[2])

    @pl.when(jnp.logical_not(is_worker))
    def _():
        drain(send.at[0:rows, 0:2], send_sem.at[0])
        drain(send.at[0:rows, 2:3], send_sem.at[1])
        drain(conv_in, land_sem.at[0])
        drain(back_in, land_sem.at[1])
        drain(corr_in, land_sem.at[2])

    @pl.when(is_worker)
    def _():
        drain(leave.at[0, 0 : peers - 1], leave_sem.at[0])
        drain(leave.at[1, 0 : peers - 1], leave_sem.at[1])

        @pl.when(foreign)
        def _():
            drain(leave.at[2], leave_sem.at[2])

        @pl.when(jnp.logical_not(foreign))
        def _():
            drain(leave.at[2, 0 : peers - 1], leave_sem.at[2])


def finish(conv_in, back_in, corr_in, direct_signal, direct_gated, cotangent, *rest):
    *results, gating_part, signal_part, filter_part, stage, sem = rest
    parts = (gating_part, signal_part, filter_part)
    lane = 128
    scale = 1.0 / math.sqrt(COARSE * FINE * corr_in.shape[1])

    def gather(values, index, last):
        part = parts[index]
        count = part.shape[0]
        stage[index, 0 : count * 8, :] = values.reshape(count * 8, lane)
        for piece in range(8):
            at = slice(piece * lane, (piece + 1) * lane)
            part[:, at] = last(stage[index, pl.ds(piece, count, stride=8), :], at).astype(part.dtype)
        pltpu.make_async_copy(part, results[index], sem.at[index]).start()

    gather(
        conv_in[...].astype(F32), 0,
        lambda value, at: cotangent[:, at].astype(F32) * (value + direct_signal[:, at]),
    )
    gather(back_in[...].astype(F32), 1, lambda value, at: value + direct_gated[:, at])
    gather(jnp.sum(corr_in[...].astype(F32), axis=1), 2, lambda value, at: value * scale)
    for index in range(3):
        pltpu.make_async_copy(parts[index], results[index], sem.at[index]).wait()


def exchange(signal, gating, cotangent, filters, skip_weight):
    rows, length = signal.shape
    total = COARSE * FINE
    peers = total // length
    operands = (signal, gating, cotangent, filters, skip_weight, *tables(total))
    vmem = pl.BlockSpec(memory_space=pltpu.VMEM)
    hbm = pl.BlockSpec(memory_space=pltpu.HBM)
    return pl.pallas_call(
        kernel,
        out_shape=(
            jax.ShapeDtypeStruct((rows, 8, 128), BF16),
            jax.ShapeDtypeStruct((rows, 8, 128), BF16),
            jax.ShapeDtypeStruct((8, 4, 8, 128), BF16),
            jax.ShapeDtypeStruct((rows, length), F32),
            jax.ShapeDtypeStruct((rows, length), F32),
            jax.ShapeDtypeStruct((rows, length), BF16),
        ),
        in_specs=[hbm] * 9,
        out_specs=(vmem,) * 6,
        scratch_shapes=[
            pltpu.VMEM((rows, length), BF16),
            pltpu.VMEM((rows, length), BF16),
            pltpu.VMEM((rows, length), F32),
            pltpu.VMEM((rows,), F32),
            pltpu.VMEM((rows, 3, 8, 128), BF16),
            pltpu.VMEM((peers, 3, 8, 128), BF16),
            pltpu.VMEM((peers * 8, 128), F32),
            pltpu.VMEM((COARSE, 2 * COARSE), BF16),
            pltpu.VMEM((COARSE, 2 * FINE), F32),
            pltpu.VMEM((2 * FINE, 2 * FINE), BF16),
            pltpu.VMEM((2 * FINE, 2 * FINE), BF16),
            pltpu.VMEM((COARSE, FINE), BF16),
            pltpu.VMEM((3, COARSE, 2 * FINE), F32),
            pltpu.VMEM((2 * COARSE, FINE), BF16),
            pltpu.VMEM((3, peers, 8, 128), BF16),
            pltpu.SemaphoreType.DMA((5,)),
            pltpu.SemaphoreType.DMA((4,)),
            pltpu.SemaphoreType.DMA((4,)),
            pltpu.SemaphoreType.DMA((2,)),
            pltpu.SemaphoreType.DMA((2,)),
            pltpu.SemaphoreType.DMA((3,)),
            pltpu.SemaphoreType.DMA((3,)),
        ],
        compiler_params=pltpu.CompilerParams(
            collective_id=0, has_side_effects=True, vmem_limit_bytes=40 * 1024 * 1024
        ),
        name="exchange",
    )(*[pltpu.with_memory_space_constraint(each, pltpu.HBM) for each in operands])


def per_device(signal, gating, cotangent, filters, skip_weight):
    rows, length = signal.shape
    landed = exchange(signal, gating, cotangent, filters, skip_weight)
    vmem = pl.BlockSpec(memory_space=pltpu.VMEM)
    grad_gating, grad_signal, grad_filters = pl.pallas_call(
        finish,
        out_shape=(
            jax.ShapeDtypeStruct((rows, length), BF16),
            jax.ShapeDtypeStruct((rows, length), BF16),
            jax.ShapeDtypeStruct((8, length), F32),
        ),
        in_specs=[vmem] * 6,
        out_specs=(pl.BlockSpec(memory_space=pl.ANY),) * 3,
        scratch_shapes=[
            pltpu.VMEM((rows, length), BF16),
            pltpu.VMEM((rows, length), BF16),
            pltpu.VMEM((8, length), F32),
            pltpu.VMEM((3, rows * 8, 128), F32),
            pltpu.SemaphoreType.DMA((3,)),
        ],
        compiler_params=pltpu.CompilerParams(vmem_limit_bytes=16 * 1024 * 1024),
        name="finish",
    )(*landed)
    return (grad_signal, grad_gating, grad_filters)


def solution(mesh):
    in_specs = (P("chan", "ctx"), P("chan", "ctx"), P("chan", "ctx"), P(None, "ctx"), P("chan"))
    out_specs = (P("chan", "ctx"), P("chan", "ctx"), P("chan", "ctx"))
    return jax.shard_map(
        per_device, mesh=mesh, in_specs=in_specs, out_specs=out_specs, check_vma=False
    )
```

```python
import math

import jax
import jax.numpy as jnp
import numpy as np
from jax import lax
from jax.experimental import pallas as pl
from jax.experimental.pallas import tpu as pltpu
from jax.sharding import PartitionSpec as P

MESH = pl.DeviceIdType.MESH
F32 = jnp.float32
BF16 = jnp.bfloat16
COARSE = 512
FAR_RING = (4, 3, 5, 2, 6, 1, 7, 0)
FAR_ROW = (2, 1, 3, 0)
FINE = 256
TILE = 256


def tables(total):
    shift = 0.25
    coarse = np.arange(COARSE) - shift
    angle = 2.0 * np.pi * ((coarse[:, None] * coarse[None, :]) / COARSE)
    big = np.concatenate([np.cos(angle), -np.sin(angle)], axis=1)
    fine = np.arange(FINE)
    angle = 2.0 * np.pi * ((coarse[:, None] * fine[None, :]) / total + coarse[:, None] * shift / COARSE)
    turn = np.concatenate([np.cos(angle), -np.sin(angle)], axis=1)
    angle = 2.0 * np.pi * ((fine[:, None] * fine[None, :]) % FINE) / FINE
    cosine, sine = np.cos(angle), np.sin(angle)
    ahead = np.block([[cosine, -sine], [sine, cosine]])
    back = np.block([[cosine, sine], [-sine, cosine]])
    as_bf16 = lambda table: jnp.asarray(table.astype(np.float32)).astype(BF16)
    return (as_bf16(big), jnp.asarray(turn.astype(np.float32)), as_bf16(ahead), as_bf16(back))


def dot(left, right):
    return jnp.dot(left, right, preferred_element_type=F32)


def kernel(
    signal_hbm, gating_hbm, cotangent_hbm, filters_hbm, weight_hbm, big_hbm, turn_hbm, ahead_hbm, back_hbm,
    conv_in, back_in, corr_in, direct_signal, direct_gated, cotangent,
    signal, gating, filters, weight, send, got, stage, big, turn, ahead, back, block, spec, mixed, leave,
    load_sem, table_sem, own_sem, send_sem, got_sem, leave_sem, land_sem,
):
    place = lax.axis_index("ctx")
    chan = lax.axis_index("chan")
    rows = 32
    peers = 128
    lane = 128
    total = COARSE * FINE
    column = place // 4
    row, ring, line = place // 32, column % 8, place % 4
    rows_at = [32 * lax.rem(row + step, 4) for step in range(4)]
    rings_at = [4 * lax.rem(ring + step, 8) for step in range(8)]
    lines_at = [lax.rem(line + step, 4) for step in range(4)]

    def worker_line(parity, channel):
        return lax.rem(1 + channel % 2 + 2 * parity, 4)

    own_parity = lax.rem(row + ring, 2)
    workers_at = [worker_line(lax.rem(own_parity + step, 2), chan) for step in range(2)]
    is_worker = line == workers_at[0]
    home = column // 8
    foreign = home != chan

    load_copies = [
        pltpu.make_async_copy(source, target, load_sem.at[index])
        for index, (source, target) in enumerate(
            (
                (signal_hbm, signal),
                (filters_hbm, filters),
                (cotangent_hbm, cotangent),
                (gating_hbm, gating),
                (weight_hbm, weight),
            )
        )
    ]
    for copy in load_copies:
        copy.start()
    table_copies = [
        pltpu.make_async_copy(big_hbm, big, table_sem.at[0]),
        pltpu.make_async_copy(turn_hbm, turn, table_sem.at[1]),
        pltpu.make_async_copy(ahead_hbm, ahead, table_sem.at[2]),
        pltpu.make_async_copy(back_hbm, back, table_sem.at[3]),
    ]

    barrier = pltpu.get_barrier_semaphore()

    def greet(ctx, other):
        pl.semaphore_signal(barrier, inc=1, device_id=(ctx, other), device_id_type=MESH)

    @pl.when(is_worker)
    def _():
        for copy in table_copies:
            copy.start()

        for ring_at in FAR_RING:
            for row_at in FAR_ROW:
                for line_at in range(4):
                    if ring_at or row_at or line_at:
                        greet(rows_at[row_at] + rings_at[ring_at] + lines_at[line_at], chan)

    for hop in range(1, 4):
        other = lax.rem(chan + hop, 4)
        others_at = [worker_line(lax.rem(chan + ring + step, 2), other) for step in range(2)]
        for ring_at in FAR_RING:
            greet(32 * chan + rings_at[ring_at] + others_at[ring_at % 2], other)

    def spread(values, kind):
        for piece in range(8):
            stage[pl.ds(piece, rows, stride=8), :] = values[:, piece * lane : (piece + 1) * lane]
        send[:, kind] = stage[0 : rows * 8, :].reshape(rows, 8, lane).astype(BF16)

    load_copies[0].wait()
    spread(signal[...].astype(F32), 0)
    load_copies[1].wait()
    spread(filters[...], 1)
    load_copies[2].wait()
    load_copies[3].wait()
    gated = (cotangent[...].astype(F32) * gating[...].astype(F32)).astype(BF16)
    spread(gated.astype(F32), 2)
    load_copies[4].wait()
    across = weight[...].reshape(1, rows) * jnp.ones((rows, 1), F32)
    diagonal = lax.broadcasted_iota(jnp.int32, (rows, rows), 0) == lax.broadcasted_iota(
        jnp.int32, (rows, rows), 1
    )
    down = jnp.sum(jnp.where(diagonal, across, 0.0), axis=1, keepdims=True)
    direct_signal[...] = down * signal[...].astype(F32)
    direct_gated[...] = down * gated.astype(F32)

    @pl.when(is_worker)
    def _():
        @pl.when(foreign)
        def _():
            pl.semaphore_wait(barrier, 31 + peers)

        @pl.when(jnp.logical_not(foreign))
        def _():
            pl.semaphore_wait(barrier, 31)

    @pl.when(jnp.logical_not(is_worker))
    def _():
        pl.semaphore_wait(barrier, 32)

    def post(index, low, high, filt, target):
        pltpu.make_async_remote_copy(
            send.at[filt, low:high], got.at[place, low:high], send_sem.at[index], got_sem.at[index],
            device_id=(target, chan), device_id_type=MESH,
        ).start()

    for index, low, high in ((0, 0, 2), (1, 2, 3)):
        for ring_at in FAR_RING:
            for row_at in FAR_ROW:
                base = rows_at[row_at] + rings_at[ring_at]
                filt = base // 4
                target = base + workers_at[(row_at + ring_at) % 2]
                if ring_at or row_at:
                    post(index, low, high, filt, target)
                else:
                    pl.when(jnp.logical_not(is_worker))(lambda: post(index, low, high, filt, target))

    def drain(ref, sem):
        pltpu.make_async_copy(ref, ref, sem).wait()

    def ahead_transform(kind):
        stage[...] = got[:, kind].astype(F32).reshape(peers * 8, lane)
        for half in range(2):
            block[:, half * lane : (half + 1) * lane] = stage[pl.ds(half, COARSE, stride=2), :].astype(BF16)

        for step in range(COARSE // TILE):
            at = pl.ds(step * TILE, TILE)
            real = dot(big[at, 0:COARSE], block[...])
            imag = dot(big[at, COARSE:], block[...])
            cosine = turn[at, 0:FINE]
            sine = turn[at, FINE:]
            turned = jnp.concatenate(
                [real * cosine - imag * sine, real * sine + imag * cosine], axis=1
            ).astype(BF16)
            spec[kind, at, :] = dot(turned, ahead[...])

    def back_transform(left, right, conjugate, kind):
        for step in range(COARSE // TILE):
            at = pl.ds(step * TILE, TILE)
            left_real = spec[left, at, 0:FINE]
            left_imag = spec[left, at, FINE:]
            right_real = spec[right, at, 0:FINE]
            right_imag = spec[right, at, FINE:]
            if conjugate:
                real = left_real * right_real + left_imag * right_imag
                imag = left_real * right_imag - left_imag * right_real
            else:
                real = left_real * right_real - left_imag * right_imag
                imag = left_real * right_imag + left_imag * right_real
            joined = jnp.concatenate([real, imag], axis=1).astype(BF16)
            half = dot(joined, back[...])
            real, imag = half[:, 0:FINE], half[:, FINE:]
            cosine = turn[at, 0:FINE]
            sine = turn[at, FINE:]
            mixed[at, :] = (real * cosine + imag * sine).astype(BF16)
            low = pl.ds(COARSE + step * TILE, TILE)
            mixed[low, :] = (imag * cosine - real * sine).astype(BF16)

        for step in range(COARSE // TILE):
            at = pl.ds(step * TILE, TILE)
            time = dot(big[at, :], mixed[...]) * (1.0 / total)
            for part in range(2):
                stage[pl.ds(2 * step * TILE + part, TILE, stride=2), :] = time[
                    :, part * lane : (part + 1) * lane
                ]

        leave[kind] = stage[...].reshape(peers, 8, lane).astype(BF16)

    def fan(one, with_self):
        @pl.loop(0, 8)
        def _(step):
            ring_at = 4 * lax.rem(ring + step, 8)
            for row_at in range(4):
                for line_at in range(4):
                    target = rows_at[row_at] + ring_at + lines_at[line_at]
                    if row_at or line_at:
                        one(target)
                    else:
                        pl.when(jnp.logical_or(step > 0, with_self))(lambda: one(target))

    def scatter(kind, landing):
        def one(target):
            pltpu.make_async_remote_copy(
                leave.at[kind, target], landing.at[column],
                leave_sem.at[kind], land_sem.at[kind],
                device_id=(target, chan), device_id_type=MESH,
            ).start()

        fan(one, False)
        pltpu.make_async_copy(leave.at[kind, place], landing.at[column], own_sem.at[1 + kind]).start()

    @pl.when(is_worker)
    def _():
        pltpu.make_async_copy(send.at[column], got.at[place], own_sem.at[0]).start()
        for copy in table_copies:
            copy.wait()
        pltpu.make_async_copy(send.at[column], got.at[place], own_sem.at[0]).wait()
        drain(got.at[0 : peers - 1, 0:2], got_sem.at[0])
        ahead_transform(0)
        ahead_transform(1)
        back_transform(0, 1, False, 0)
        scatter(0, conv_in)
        drain(got.at[0 : peers - 1, 2:3], got_sem.at[1])
        ahead_transform(2)
        back_transform(0, 2, True, 2)

        def send_home(target):
            pltpu.make_async_remote_copy(
                leave.at[2, target], corr_in.at[column % 8, chan],
                leave_sem.at[2], land_sem.at[2],
                device_id=(target, home), device_id_type=MESH,
            ).start()

        fan(send_home, foreign)

        @pl.when(jnp.logical_not(foreign))
        def _():
            pltpu.make_async_copy(leave.at[2, place], corr_in.at[column % 8, chan], own_sem.at[3]).start()

        back_transform(1, 2, True, 1)
        scatter(1, back_in)

        drain(send.at[0 : rows - 1, 0:2], send_sem.at[0])
        drain(send.at[0 : rows - 1, 2:3], send_sem.at[1])
        for kind, landing in ((0, conv_in), (1, back_in)):
            pltpu.make_async_copy(leave.at[kind, place], landing.at[column], own_sem.at[1 + kind]).wait()
            drain(landing.at[0 : rows - 1], land_sem.at[kind])

        @pl.when(foreign)
        def _():
            drain(corr_in, land_sem.at[2])

        @pl.when(jnp.logical_not(foreign))
        def _():
            pltpu.make_async_copy(leave.at[2, place], corr_in.at[column % 8, chan], own_sem.at[3]).wait()
            drain(leave.at[2, 0 : rows - 1], land_sem.at[2])

    @pl.when(jnp.logical_not(is_worker))
    def _():
        drain(send.at[0:rows, 0:2], send_sem.at[0])
        drain(send.at[0:rows, 2:3], send_sem.at[1])
        drain(conv_in, land_sem.at[0])
        drain(back_in, land_sem.at[1])
        drain(corr_in, land_sem.at[2])

    @pl.when(is_worker)
    def _():
        drain(leave.at[0, 0 : peers - 1], leave_sem.at[0])
        drain(leave.at[1, 0 : peers - 1], leave_sem.at[1])

        @pl.when(foreign)
        def _():
            drain(leave.at[2], leave_sem.at[2])

        @pl.when(jnp.logical_not(foreign))
        def _():
            drain(leave.at[2, 0 : peers - 1], leave_sem.at[2])


def finish(conv_in, back_in, corr_in, direct_signal, direct_gated, cotangent, *rest):
    *results, gating_part, signal_part, filter_part, stage, sem = rest
    parts = (gating_part, signal_part, filter_part)
    lane = 128
    scale = 1.0 / math.sqrt(COARSE * FINE * corr_in.shape[1])

    def gather(values, index, last):
        part = parts[index]
        count = part.shape[0]
        stage[index, 0 : count * 8, :] = values.reshape(count * 8, lane)
        for piece in range(8):
            at = slice(piece * lane, (piece + 1) * lane)
            part[:, at] = last(stage[index, pl.ds(piece, count, stride=8), :], at).astype(part.dtype)
        pltpu.make_async_copy(part, results[index], sem.at[index]).start()

    gather(
        conv_in[...].astype(F32), 0,
        lambda value, at: cotangent[:, at].astype(F32) * (value + direct_signal[:, at]),
    )
    gather(back_in[...].astype(F32), 1, lambda value, at: value + direct_gated[:, at])
    gather(jnp.sum(corr_in[...].astype(F32), axis=1), 2, lambda value, at: value * scale)
    for index in range(3):
        pltpu.make_async_copy(parts[index], results[index], sem.at[index]).wait()


def exchange(signal, gating, cotangent, filters, skip_weight):
    rows, length = signal.shape
    total = COARSE * FINE
    peers = total // length
    operands = (signal, gating, cotangent, filters, skip_weight, *tables(total))
    vmem = pl.BlockSpec(memory_space=pltpu.VMEM)
    hbm = pl.BlockSpec(memory_space=pltpu.HBM)
    return pl.pallas_call(
        kernel,
        out_shape=(
            jax.ShapeDtypeStruct((rows, 8, 128), BF16),
            jax.ShapeDtypeStruct((rows, 8, 128), BF16),
            jax.ShapeDtypeStruct((8, 4, 8, 128), BF16),
            jax.ShapeDtypeStruct((rows, length), F32),
            jax.ShapeDtypeStruct((rows, length), F32),
            jax.ShapeDtypeStruct((rows, length), BF16),
        ),
        in_specs=[hbm] * 9,
        out_specs=(vmem,) * 6,
        scratch_shapes=[
            pltpu.VMEM((rows, length), BF16),
            pltpu.VMEM((rows, length), BF16),
            pltpu.VMEM((rows, length), F32),
            pltpu.VMEM((rows,), F32),
            pltpu.VMEM((rows, 3, 8, 128), BF16),
            pltpu.VMEM((peers, 3, 8, 128), BF16),
            pltpu.VMEM((peers * 8, 128), F32),
            pltpu.VMEM((COARSE, 2 * COARSE), BF16),
            pltpu.VMEM((COARSE, 2 * FINE), F32),
            pltpu.VMEM((2 * FINE, 2 * FINE), BF16),
            pltpu.VMEM((2 * FINE, 2 * FINE), BF16),
            pltpu.VMEM((COARSE, FINE), BF16),
            pltpu.VMEM((3, COARSE, 2 * FINE), F32),
            pltpu.VMEM((2 * COARSE, FINE), BF16),
            pltpu.VMEM((3, peers, 8, 128), BF16),
            pltpu.SemaphoreType.DMA((5,)),
            pltpu.SemaphoreType.DMA((4,)),
            pltpu.SemaphoreType.DMA((4,)),
            pltpu.SemaphoreType.DMA((2,)),
            pltpu.SemaphoreType.DMA((2,)),
            pltpu.SemaphoreType.DMA((3,)),
            pltpu.SemaphoreType.DMA((3,)),
        ],
        compiler_params=pltpu.CompilerParams(
            collective_id=0, has_side_effects=True, vmem_limit_bytes=40 * 1024 * 1024
        ),
        name="exchange",
    )(*[pltpu.with_memory_space_constraint(each, pltpu.HBM) for each in operands])


def per_device(signal, gating, cotangent, filters, skip_weight):
    rows, length = signal.shape
    landed = exchange(signal, gating, cotangent, filters, skip_weight)
    vmem = pl.BlockSpec(memory_space=pltpu.VMEM)
    grad_gating, grad_signal, grad_filters = pl.pallas_call(
        finish,
        out_shape=(
            jax.ShapeDtypeStruct((rows, length), BF16),
            jax.ShapeDtypeStruct((rows, length), BF16),
            jax.ShapeDtypeStruct((8, length), F32),
        ),
        in_specs=[vmem] * 6,
        out_specs=(pl.BlockSpec(memory_space=pl.ANY),) * 3,
        scratch_shapes=[
            pltpu.VMEM((rows, length), BF16),
            pltpu.VMEM((rows, length), BF16),
            pltpu.VMEM((8, length), F32),
            pltpu.VMEM((3, rows * 8, 128), F32),
            pltpu.SemaphoreType.DMA((3,)),
        ],
        compiler_params=pltpu.CompilerParams(vmem_limit_bytes=16 * 1024 * 1024),
        name="finish",
    )(*landed)
    return (grad_signal, grad_gating, grad_filters)


def solution(mesh):
    in_specs = (P("chan", "ctx"), P("chan", "ctx"), P("chan", "ctx"), P(None, "ctx"), P("chan"))
    out_specs = (P("chan", "ctx"), P("chan", "ctx"), P("chan", "ctx"))
    return jax.shard_map(
        per_device, mesh=mesh, in_specs=in_specs, out_specs=out_specs, check_vma=False
    )
```

```python
import math

import jax
import jax.numpy as jnp
import numpy as np
from jax import lax
from jax.experimental import pallas as pl
from jax.experimental.pallas import tpu as pltpu
from jax.sharding import PartitionSpec as P

MESH = pl.DeviceIdType.MESH
F32 = jnp.float32
BF16 = jnp.bfloat16
COARSE = 512
FAR_RING = (4, 3, 5, 2, 6, 1, 7, 0)
FAR_ROW = (2, 1, 3, 0)
FINE = 256
TILE = 256


def tables(total):
    shift = 0.25
    coarse = np.arange(COARSE) - shift
    angle = 2.0 * np.pi * ((coarse[:, None] * coarse[None, :]) / COARSE)
    big = np.concatenate([np.cos(angle), -np.sin(angle)], axis=1)
    fine = np.arange(FINE)
    angle = 2.0 * np.pi * ((coarse[:, None] * fine[None, :]) / total + coarse[:, None] * shift / COARSE)
    turn = np.concatenate([np.cos(angle), -np.sin(angle)], axis=1)
    angle = 2.0 * np.pi * ((fine[:, None] * fine[None, :]) % FINE) / FINE
    cosine, sine = np.cos(angle), np.sin(angle)
    ahead = np.block([[cosine, -sine], [sine, cosine]])
    back = np.block([[cosine, sine], [-sine, cosine]])
    as_bf16 = lambda table: jnp.asarray(table.astype(np.float32)).astype(BF16)
    return (as_bf16(big), jnp.asarray(turn.astype(np.float32)), as_bf16(ahead), as_bf16(back))


def dot(left, right):
    return jnp.dot(left, right, preferred_element_type=F32)


def kernel(
    signal_hbm, gating_hbm, cotangent_hbm, filters_hbm, weight_hbm, big_hbm, turn_hbm, ahead_hbm, back_hbm,
    conv_in, back_in, corr_in, direct_signal, direct_gated, cotangent,
    signal, gating, filters, weight, send, got, stage, big, turn, ahead, back, block, spec, mixed, leave,
    load_sem, table_sem, own_sem, send_sem, got_sem, leave_sem, land_sem,
):
    place = lax.axis_index("ctx")
    chan = lax.axis_index("chan")
    rows = 32
    peers = 128
    lane = 128
    total = COARSE * FINE
    column = place // 4
    row, ring, line = place // 32, column % 8, place % 4
    rows_at = [32 * lax.rem(row + step, 4) for step in range(4)]
    rings_at = [4 * lax.rem(ring + step, 8) for step in range(8)]
    lines_at = [lax.rem(line + step, 4) for step in range(4)]

    def worker_line(parity, channel):
        return 3 * lax.rem(channel, 2) + (1 - 2 * lax.rem(channel, 2)) * (1 - parity)

    own_parity = lax.rem(row + ring, 2)
    workers_at = [worker_line(lax.rem(own_parity + step, 2), chan) for step in range(2)]
    is_worker = line == workers_at[0]
    home = column // 8
    foreign = home != chan

    load_copies = [
        pltpu.make_async_copy(source, target, load_sem.at[index])
        for index, (source, target) in enumerate(
            (
                (signal_hbm, signal),
                (filters_hbm, filters),
                (cotangent_hbm, cotangent),
                (gating_hbm, gating),
                (weight_hbm, weight),
            )
        )
    ]
    for copy in load_copies:
        copy.start()
    table_copies = [
        pltpu.make_async_copy(big_hbm, big, table_sem.at[0]),
        pltpu.make_async_copy(turn_hbm, turn, table_sem.at[1]),
        pltpu.make_async_copy(ahead_hbm, ahead, table_sem.at[2]),
        pltpu.make_async_copy(back_hbm, back, table_sem.at[3]),
    ]

    barrier = pltpu.get_barrier_semaphore()

    def greet(ctx, other):
        pl.semaphore_signal(barrier, inc=1, device_id=(ctx, other), device_id_type=MESH)

    @pl.when(is_worker)
    def _():
        for copy in table_copies:
            copy.start()

        for ring_at in FAR_RING:
            for row_at in FAR_ROW:
                for line_at in range(4):
                    if ring_at or row_at or line_at:
                        greet(rows_at[row_at] + rings_at[ring_at] + lines_at[line_at], chan)

    for hop in range(1, 4):
        other = lax.rem(chan + hop, 4)
        others_at = [worker_line(lax.rem(chan + ring + step, 2), other) for step in range(2)]
        for ring_at in FAR_RING:
            greet(32 * chan + rings_at[ring_at] + others_at[ring_at % 2], other)

    def spread(values, kind):
        for piece in range(8):
            stage[pl.ds(piece, rows, stride=8), :] = values[:, piece * lane : (piece + 1) * lane]
        send[:, kind] = stage[0 : rows * 8, :].reshape(rows, 8, lane).astype(BF16)

    load_copies[0].wait()
    spread(signal[...].astype(F32), 0)
    load_copies[1].wait()
    spread(filters[...], 1)
    load_copies[2].wait()
    load_copies[3].wait()
    gated = (cotangent[...].astype(F32) * gating[...].astype(F32)).astype(BF16)
    spread(gated.astype(F32), 2)
    load_copies[4].wait()
    across = weight[...].reshape(1, rows) * jnp.ones((rows, 1), F32)
    diagonal = lax.broadcasted_iota(jnp.int32, (rows, rows), 0) == lax.broadcasted_iota(
        jnp.int32, (rows, rows), 1
    )
    down = jnp.sum(jnp.where(diagonal, across, 0.0), axis=1, keepdims=True)
    direct_signal[...] = down * signal[...].astype(F32)
    direct_gated[...] = down * gated.astype(F32)

    @pl.when(is_worker)
    def _():
        @pl.when(foreign)
        def _():
            pl.semaphore_wait(barrier, 31 + peers)

        @pl.when(jnp.logical_not(foreign))
        def _():
            pl.semaphore_wait(barrier, 31)

    @pl.when(jnp.logical_not(is_worker))
    def _():
        pl.semaphore_wait(barrier, 32)

    def post(index, low, high, filt, target):
        pltpu.make_async_remote_copy(
            send.at[filt, low:high], got.at[place, low:high], send_sem.at[index], got_sem.at[index],
            device_id=(target, chan), device_id_type=MESH,
        ).start()

    for index, low, high in ((0, 0, 2), (1, 2, 3)):
        for ring_at in FAR_RING:
            for row_at in FAR_ROW:
                base = rows_at[row_at] + rings_at[ring_at]
                filt = base // 4
                target = base + workers_at[(row_at + ring_at) % 2]
                if ring_at or row_at:
                    post(index, low, high, filt, target)
                else:
                    pl.when(jnp.logical_not(is_worker))(lambda: post(index, low, high, filt, target))

    def drain(ref, sem):
        pltpu.make_async_copy(ref, ref, sem).wait()

    def ahead_transform(kind):
        stage[...] = got[:, kind].astype(F32).reshape(peers * 8, lane)
        for half in range(2):
            block[:, half * lane : (half + 1) * lane] = stage[pl.ds(half, COARSE, stride=2), :].astype(BF16)

        for step in range(COARSE // TILE):
            at = pl.ds(step * TILE, TILE)
            real = dot(big[at, 0:COARSE], block[...])
            imag = dot(big[at, COARSE:], block[...])
            cosine = turn[at, 0:FINE]
            sine = turn[at, FINE:]
            turned = jnp.concatenate(
                [real * cosine - imag * sine, real * sine + imag * cosine], axis=1
            ).astype(BF16)
            spec[kind, at, :] = dot(turned, ahead[...])

    def back_transform(left, right, conjugate, kind):
        for step in range(COARSE // TILE):
            at = pl.ds(step * TILE, TILE)
            left_real = spec[left, at, 0:FINE]
            left_imag = spec[left, at, FINE:]
            right_real = spec[right, at, 0:FINE]
            right_imag = spec[right, at, FINE:]
            if conjugate:
                real = left_real * right_real + left_imag * right_imag
                imag = left_real * right_imag - left_imag * right_real
            else:
                real = left_real * right_real - left_imag * right_imag
                imag = left_real * right_imag + left_imag * right_real
            joined = jnp.concatenate([real, imag], axis=1).astype(BF16)
            half = dot(joined, back[...])
            real, imag = half[:, 0:FINE], half[:, FINE:]
            cosine = turn[at, 0:FINE]
            sine = turn[at, FINE:]
            mixed[at, :] = (real * cosine + imag * sine).astype(BF16)
            low = pl.ds(COARSE + step * TILE, TILE)
            mixed[low, :] = (imag * cosine - real * sine).astype(BF16)

        for step in range(COARSE // TILE):
            at = pl.ds(step * TILE, TILE)
            time = dot(big[at, :], mixed[...]) * (1.0 / total)
            for part in range(2):
                stage[pl.ds(2 * step * TILE + part, TILE, stride=2), :] = time[
                    :, part * lane : (part + 1) * lane
                ]

        leave[kind] = stage[...].reshape(peers, 8, lane).astype(BF16)

    def fan(one, with_self):
        for row_at in FAR_ROW:
            for ring_at in FAR_RING:
                for line_at in range(4):
                    target = rows_at[row_at] + rings_at[ring_at] + lines_at[line_at]
                    if ring_at or line_at or row_at:
                        one(target)
                    else:
                        pl.when(with_self)(lambda: one(target))

    def scatter(kind, landing):
        def one(target):
            pltpu.make_async_remote_copy(
                leave.at[kind, target], landing.at[column],
                leave_sem.at[kind], land_sem.at[kind],
                device_id=(target, chan), device_id_type=MESH,
            ).start()

        fan(one, False)
        pltpu.make_async_copy(leave.at[kind, place], landing.at[column], own_sem.at[1 + kind]).start()

    @pl.when(is_worker)
    def _():
        pltpu.make_async_copy(send.at[column], got.at[place], own_sem.at[0]).start()
        for copy in table_copies:
            copy.wait()
        pltpu.make_async_copy(send.at[column], got.at[place], own_sem.at[0]).wait()
        drain(got.at[0 : peers - 1, 0:2], got_sem.at[0])
        ahead_transform(0)
        ahead_transform(1)
        back_transform(0, 1, False, 0)
        scatter(0, conv_in)
        drain(got.at[0 : peers - 1, 2:3], got_sem.at[1])
        ahead_transform(2)
        back_transform(0, 2, True, 2)

        def send_home(target):
            pltpu.make_async_remote_copy(
                leave.at[2, target], corr_in.at[column % 8, chan],
                leave_sem.at[2], land_sem.at[2],
                device_id=(target, home), device_id_type=MESH,
            ).start()

        fan(send_home, foreign)

        @pl.when(jnp.logical_not(foreign))
        def _():
            pltpu.make_async_copy(leave.at[2, place], corr_in.at[column % 8, chan], own_sem.at[3]).start()

        back_transform(1, 2, True, 1)
        scatter(1, back_in)

        drain(send.at[0 : rows - 1, 0:2], send_sem.at[0])
        drain(send.at[0 : rows - 1, 2:3], send_sem.at[1])
        for kind, landing in ((0, conv_in), (1, back_in)):
            pltpu.make_async_copy(leave.at[kind, place], landing.at[column], own_sem.at[1 + kind]).wait()
            drain(landing.at[0 : rows - 1], land_sem.at[kind])

        @pl.when(foreign)
        def _():
            drain(corr_in, land_sem.at[2])

        @pl.when(jnp.logical_not(foreign))
        def _():
            pltpu.make_async_copy(leave.at[2, place], corr_in.at[column % 8, chan], own_sem.at[3]).wait()
            drain(leave.at[2, 0 : rows - 1], land_sem.at[2])

    @pl.when(jnp.logical_not(is_worker))
    def _():
        drain(send.at[0:rows, 0:2], send_sem.at[0])
        drain(send.at[0:rows, 2:3], send_sem.at[1])
        drain(conv_in, land_sem.at[0])
        drain(back_in, land_sem.at[1])
        drain(corr_in, land_sem.at[2])

    @pl.when(is_worker)
    def _():
        drain(leave.at[0, 0 : peers - 1], leave_sem.at[0])
        drain(leave.at[1, 0 : peers - 1], leave_sem.at[1])

        @pl.when(foreign)
        def _():
            drain(leave.at[2], leave_sem.at[2])

        @pl.when(jnp.logical_not(foreign))
        def _():
            drain(leave.at[2, 0 : peers - 1], leave_sem.at[2])


def finish(conv_in, back_in, corr_in, direct_signal, direct_gated, cotangent, *rest):
    *results, gating_part, signal_part, filter_part, stage, sem = rest
    parts = (gating_part, signal_part, filter_part)
    lane = 128
    scale = 1.0 / math.sqrt(COARSE * FINE * corr_in.shape[1])

    def gather(values, index, last):
        part = parts[index]
        count = part.shape[0]
        stage[index, 0 : count * 8, :] = values.reshape(count * 8, lane)
        for piece in range(8):
            at = slice(piece * lane, (piece + 1) * lane)
            part[:, at] = last(stage[index, pl.ds(piece, count, stride=8), :], at).astype(part.dtype)
        pltpu.make_async_copy(part, results[index], sem.at[index]).start()

    gather(
        conv_in[...].astype(F32), 0,
        lambda value, at: cotangent[:, at].astype(F32) * (value + direct_signal[:, at]),
    )
    gather(back_in[...].astype(F32), 1, lambda value, at: value + direct_gated[:, at])
    gather(jnp.sum(corr_in[...].astype(F32), axis=1), 2, lambda value, at: value * scale)
    for index in range(3):
        pltpu.make_async_copy(parts[index], results[index], sem.at[index]).wait()


def exchange(signal, gating, cotangent, filters, skip_weight):
    rows, length = signal.shape
    total = COARSE * FINE
    peers = total // length
    operands = (signal, gating, cotangent, filters, skip_weight, *tables(total))
    vmem = pl.BlockSpec(memory_space=pltpu.VMEM)
    hbm = pl.BlockSpec(memory_space=pltpu.HBM)
    return pl.pallas_call(
        kernel,
        out_shape=(
            jax.ShapeDtypeStruct((rows, 8, 128), BF16),
            jax.ShapeDtypeStruct((rows, 8, 128), BF16),
            jax.ShapeDtypeStruct((8, 4, 8, 128), BF16),
            jax.ShapeDtypeStruct((rows, length), F32),
            jax.ShapeDtypeStruct((rows, length), F32),
            jax.ShapeDtypeStruct((rows, length), BF16),
        ),
        in_specs=[hbm] * 9,
        out_specs=(vmem,) * 6,
        scratch_shapes=[
            pltpu.VMEM((rows, length), BF16),
            pltpu.VMEM((rows, length), BF16),
            pltpu.VMEM((rows, length), F32),
            pltpu.VMEM((rows,), F32),
            pltpu.VMEM((rows, 3, 8, 128), BF16),
            pltpu.VMEM((peers, 3, 8, 128), BF16),
            pltpu.VMEM((peers * 8, 128), F32),
            pltpu.VMEM((COARSE, 2 * COARSE), BF16),
            pltpu.VMEM((COARSE, 2 * FINE), F32),
            pltpu.VMEM((2 * FINE, 2 * FINE), BF16),
            pltpu.VMEM((2 * FINE, 2 * FINE), BF16),
            pltpu.VMEM((COARSE, FINE), BF16),
            pltpu.VMEM((3, COARSE, 2 * FINE), F32),
            pltpu.VMEM((2 * COARSE, FINE), BF16),
            pltpu.VMEM((3, peers, 8, 128), BF16),
            pltpu.SemaphoreType.DMA((5,)),
            pltpu.SemaphoreType.DMA((4,)),
            pltpu.SemaphoreType.DMA((4,)),
            pltpu.SemaphoreType.DMA((2,)),
            pltpu.SemaphoreType.DMA((2,)),
            pltpu.SemaphoreType.DMA((3,)),
            pltpu.SemaphoreType.DMA((3,)),
        ],
        compiler_params=pltpu.CompilerParams(
            collective_id=0, has_side_effects=True, vmem_limit_bytes=40 * 1024 * 1024
        ),
        name="exchange",
    )(*[pltpu.with_memory_space_constraint(each, pltpu.HBM) for each in operands])


def per_device(signal, gating, cotangent, filters, skip_weight):
    rows, length = signal.shape
    landed = exchange(signal, gating, cotangent, filters, skip_weight)
    vmem = pl.BlockSpec(memory_space=pltpu.VMEM)
    grad_gating, grad_signal, grad_filters = pl.pallas_call(
        finish,
        out_shape=(
            jax.ShapeDtypeStruct((rows, length), BF16),
            jax.ShapeDtypeStruct((rows, length), BF16),
            jax.ShapeDtypeStruct((8, length), F32),
        ),
        in_specs=[vmem] * 6,
        out_specs=(pl.BlockSpec(memory_space=pl.ANY),) * 3,
        scratch_shapes=[
            pltpu.VMEM((rows, length), BF16),
            pltpu.VMEM((rows, length), BF16),
            pltpu.VMEM((8, length), F32),
            pltpu.VMEM((3, rows * 8, 128), F32),
            pltpu.SemaphoreType.DMA((3,)),
        ],
        compiler_params=pltpu.CompilerParams(vmem_limit_bytes=16 * 1024 * 1024),
        name="finish",
    )(*landed)
    return (grad_signal, grad_gating, grad_filters)


def solution(mesh):
    in_specs = (P("chan", "ctx"), P("chan", "ctx"), P("chan", "ctx"), P(None, "ctx"), P("chan"))
    out_specs = (P("chan", "ctx"), P("chan", "ctx"), P("chan", "ctx"))
    return jax.shard_map(
        per_device, mesh=mesh, in_specs=in_specs, out_specs=out_specs, check_vma=False
    )
```

```python
import math

import jax
import jax.numpy as jnp
import numpy as np
from jax import lax
from jax.experimental import pallas as pl
from jax.experimental.pallas import tpu as pltpu
from jax.sharding import PartitionSpec as P

MESH = pl.DeviceIdType.MESH
F32 = jnp.float32
BF16 = jnp.bfloat16
COARSE = 512
FAR_RING = (4, 3, 5, 2, 6, 1, 7, 0)
FAR_ROW = (2, 1, 3, 0)
FINE = 256
TILE = 256


def tables(total):
    shift = 0.25
    coarse = np.arange(COARSE) - shift
    angle = 2.0 * np.pi * ((coarse[:, None] * coarse[None, :]) / COARSE)
    big = np.concatenate([np.cos(angle), -np.sin(angle)], axis=1)
    fine = np.arange(FINE)
    angle = 2.0 * np.pi * ((coarse[:, None] * fine[None, :]) / total + coarse[:, None] * shift / COARSE)
    turn = np.concatenate([np.cos(angle), -np.sin(angle)], axis=1)
    angle = 2.0 * np.pi * ((fine[:, None] * fine[None, :]) % FINE) / FINE
    cosine, sine = np.cos(angle), np.sin(angle)
    ahead = np.block([[cosine, -sine], [sine, cosine]])
    back = np.block([[cosine, sine], [-sine, cosine]])
    as_bf16 = lambda table: jnp.asarray(table.astype(np.float32)).astype(BF16)
    return (as_bf16(big), jnp.asarray(turn.astype(np.float32)), as_bf16(ahead), as_bf16(back))


def dot(left, right):
    return jnp.dot(left, right, preferred_element_type=F32)


def kernel(
    signal_hbm, gating_hbm, cotangent_hbm, filters_hbm, weight_hbm, big_hbm, turn_hbm, ahead_hbm, back_hbm,
    conv_in, back_in, corr_in, direct_signal, direct_gated, cotangent,
    signal, gating, filters, weight, send, got, stage, big, turn, ahead, back, block, spec, mixed, leave,
    load_sem, table_sem, own_sem, send_sem, got_sem, leave_sem, land_sem,
):
    place = lax.axis_index("ctx")
    chan = lax.axis_index("chan")
    rows = 32
    peers = 128
    lane = 128
    total = COARSE * FINE
    column = place // 4
    row, ring, line = place // 32, column % 8, place % 4
    rows_at = [32 * lax.rem(row + step, 4) for step in range(4)]
    rings_at = [4 * lax.rem(ring + step, 8) for step in range(8)]
    lines_at = [lax.rem(line + step, 4) for step in range(4)]

    def worker_line(parity, channel):
        return 3 * lax.rem(channel, 2) + (1 - 2 * lax.rem(channel, 2)) * (1 - parity)

    own_parity = lax.rem(row + ring, 2)
    workers_at = [worker_line(lax.rem(own_parity + step, 2), chan) for step in range(2)]
    is_worker = line == workers_at[0]
    home = column // 8
    foreign = home != chan

    load_copies = [
        pltpu.make_async_copy(source, target, load_sem.at[index])
        for index, (source, target) in enumerate(
            (
                (signal_hbm, signal),
                (filters_hbm, filters),
                (cotangent_hbm, cotangent),
                (gating_hbm, gating),
                (weight_hbm, weight),
            )
        )
    ]
    for copy in load_copies:
        copy.start()
    table_copies = [
        pltpu.make_async_copy(big_hbm, big, table_sem.at[0]),
        pltpu.make_async_copy(turn_hbm, turn, table_sem.at[1]),
        pltpu.make_async_copy(ahead_hbm, ahead, table_sem.at[2]),
        pltpu.make_async_copy(back_hbm, back, table_sem.at[3]),
    ]

    barrier = pltpu.get_barrier_semaphore()

    def greet(ctx, other):
        pl.semaphore_signal(barrier, inc=1, device_id=(ctx, other), device_id_type=MESH)

    @pl.when(is_worker)
    def _():
        for copy in table_copies:
            copy.start()

        for ring_at in FAR_RING:
            for row_at in FAR_ROW:
                for line_at in range(4):
                    if ring_at or row_at or line_at:
                        greet(rows_at[row_at] + rings_at[ring_at] + lines_at[line_at], chan)

    for hop in range(1, 4):
        other = lax.rem(chan + hop, 4)
        others_at = [worker_line(lax.rem(chan + ring + step, 2), other) for step in range(2)]
        for ring_at in FAR_RING:
            greet(32 * chan + rings_at[ring_at] + others_at[ring_at % 2], other)

    def spread(values, kind):
        for piece in range(8):
            stage[pl.ds(piece, rows, stride=8), :] = values[:, piece * lane : (piece + 1) * lane]
        send[:, kind] = stage[0 : rows * 8, :].reshape(rows, 8, lane).astype(BF16)

    load_copies[0].wait()
    spread(signal[...].astype(F32), 0)
    load_copies[1].wait()
    spread(filters[...], 1)
    load_copies[2].wait()
    load_copies[3].wait()
    gated = (cotangent[...].astype(F32) * gating[...].astype(F32)).astype(BF16)
    spread(gated.astype(F32), 2)
    load_copies[4].wait()
    across = weight[...].reshape(1, rows) * jnp.ones((rows, 1), F32)
    diagonal = lax.broadcasted_iota(jnp.int32, (rows, rows), 0) == lax.broadcasted_iota(
        jnp.int32, (rows, rows), 1
    )
    down = jnp.sum(jnp.where(diagonal, across, 0.0), axis=1, keepdims=True)
    direct_signal[...] = down * signal[...].astype(F32)
    direct_gated[...] = down * gated.astype(F32)

    @pl.when(is_worker)
    def _():
        @pl.when(foreign)
        def _():
            pl.semaphore_wait(barrier, 31 + peers)

        @pl.when(jnp.logical_not(foreign))
        def _():
            pl.semaphore_wait(barrier, 31)

    @pl.when(jnp.logical_not(is_worker))
    def _():
        pl.semaphore_wait(barrier, 32)

    def post(index, low, high, filt, target):
        pltpu.make_async_remote_copy(
            send.at[filt, low:high], got.at[place, low:high], send_sem.at[index], got_sem.at[index],
            device_id=(target, chan), device_id_type=MESH,
        ).start()

    for index, low, high in ((0, 0, 2), (1, 2, 3)):
        for ring_at in FAR_RING:
            for row_at in FAR_ROW:
                base = rows_at[row_at] + rings_at[ring_at]
                filt = base // 4
                target = base + workers_at[(row_at + ring_at) % 2]
                if ring_at or row_at:
                    post(index, low, high, filt, target)
                else:
                    pl.when(jnp.logical_not(is_worker))(lambda: post(index, low, high, filt, target))

    def drain(ref, sem):
        pltpu.make_async_copy(ref, ref, sem).wait()

    def ahead_transform(kind):
        stage[...] = got[:, kind].astype(F32).reshape(peers * 8, lane)
        for half in range(2):
            block[:, half * lane : (half + 1) * lane] = stage[pl.ds(half, COARSE, stride=2), :].astype(BF16)

        for step in range(COARSE // TILE):
            at = pl.ds(step * TILE, TILE)
            real = dot(big[at, 0:COARSE], block[...])
            imag = dot(big[at, COARSE:], block[...])
            cosine = turn[at, 0:FINE]
            sine = turn[at, FINE:]
            turned = jnp.concatenate(
                [real * cosine - imag * sine, real * sine + imag * cosine], axis=1
            ).astype(BF16)
            spec[kind, at, :] = dot(turned, ahead[...])

    def back_transform(left, right, conjugate, kind, after=None):
        for step in range(COARSE // TILE):
            at = pl.ds(step * TILE, TILE)
            left_real = spec[left, at, 0:FINE]
            left_imag = spec[left, at, FINE:]
            right_real = spec[right, at, 0:FINE]
            right_imag = spec[right, at, FINE:]
            if conjugate:
                real = left_real * right_real + left_imag * right_imag
                imag = left_real * right_imag - left_imag * right_real
            else:
                real = left_real * right_real - left_imag * right_imag
                imag = left_real * right_imag + left_imag * right_real
            joined = jnp.concatenate([real, imag], axis=1).astype(BF16)
            half = dot(joined, back[...])
            real, imag = half[:, 0:FINE], half[:, FINE:]
            cosine = turn[at, 0:FINE]
            sine = turn[at, FINE:]
            mixed[at, :] = (real * cosine + imag * sine).astype(BF16)
            low = pl.ds(COARSE + step * TILE, TILE)
            mixed[low, :] = (imag * cosine - real * sine).astype(BF16)

        for step in range(COARSE // TILE):
            at = pl.ds(step * TILE, TILE)
            time = dot(big[at, :], mixed[...]) * (1.0 / total)
            for part in range(2):
                stage[pl.ds(2 * step * TILE + part, TILE, stride=2), :] = time[
                    :, part * lane : (part + 1) * lane
                ]

            if after is not None:
                half = peers * TILE // COARSE
                leave[kind, step * half : (step + 1) * half] = (
                    stage[2 * step * TILE : 2 * (step + 1) * TILE, :].reshape(half, 8, lane).astype(BF16)
                )
                after(step)

        if after is None:
            leave[kind] = stage[...].reshape(peers, 8, lane).astype(BF16)

    def fan(one, with_self):
        for row_at in FAR_ROW:
            for ring_at in FAR_RING:
                for line_at in range(4):
                    target = rows_at[row_at] + rings_at[ring_at] + lines_at[line_at]
                    if ring_at or line_at or row_at:
                        one(target)
                    else:
                        pl.when(with_self)(lambda: one(target))

    def scatter(kind, landing):
        def one(target):
            pltpu.make_async_remote_copy(
                leave.at[kind, target], landing.at[column],
                leave_sem.at[kind], land_sem.at[kind],
                device_id=(target, chan), device_id_type=MESH,
            ).start()

        fan(one, False)
        pltpu.make_async_copy(leave.at[kind, place], landing.at[column], own_sem.at[1 + kind]).start()

    @pl.when(is_worker)
    def _():
        pltpu.make_async_copy(send.at[column], got.at[place], own_sem.at[0]).start()
        for copy in table_copies:
            copy.wait()
        pltpu.make_async_copy(send.at[column], got.at[place], own_sem.at[0]).wait()
        drain(got.at[0 : peers - 1, 0:2], got_sem.at[0])
        ahead_transform(0)
        ahead_transform(1)
        back_transform(0, 1, False, 0)
        scatter(0, conv_in)
        drain(got.at[0 : peers - 1, 2:3], got_sem.at[1])
        ahead_transform(2)
        back_transform(0, 2, True, 2)

        def send_home(target):
            pltpu.make_async_remote_copy(
                leave.at[2, target], corr_in.at[column % 8, chan],
                leave_sem.at[2], land_sem.at[2],
                device_id=(target, home), device_id_type=MESH,
            ).start()

        fan(send_home, foreign)

        @pl.when(jnp.logical_not(foreign))
        def _():
            pltpu.make_async_copy(leave.at[2, place], corr_in.at[column % 8, chan], own_sem.at[3]).start()

        def send_half(step):
            for ring_at in FAR_RING:
                for row_at in (2 * step, 2 * step + 1):
                    for line_at in range(4):
                        target = 32 * row_at + rings_at[ring_at] + lines_at[line_at]
                        if ring_at or line_at:
                            send_back(target)
                        else:
                            pl.when(row != row_at)(lambda: send_back(target))

        def send_back(target):
            pltpu.make_async_remote_copy(
                leave.at[1, target], back_in.at[column],
                leave_sem.at[1], land_sem.at[1],
                device_id=(target, chan), device_id_type=MESH,
            ).start()

        back_transform(1, 2, True, 1, send_half)
        pltpu.make_async_copy(leave.at[1, place], back_in.at[column], own_sem.at[2]).start()

        drain(send.at[0 : rows - 1, 0:2], send_sem.at[0])
        drain(send.at[0 : rows - 1, 2:3], send_sem.at[1])
        for kind, landing in ((0, conv_in), (1, back_in)):
            pltpu.make_async_copy(leave.at[kind, place], landing.at[column], own_sem.at[1 + kind]).wait()
            drain(landing.at[0 : rows - 1], land_sem.at[kind])

        @pl.when(foreign)
        def _():
            drain(corr_in, land_sem.at[2])

        @pl.when(jnp.logical_not(foreign))
        def _():
            pltpu.make_async_copy(leave.at[2, place], corr_in.at[column % 8, chan], own_sem.at[3]).wait()
            drain(leave.at[2, 0 : rows - 1], land_sem.at[2])

    @pl.when(jnp.logical_not(is_worker))
    def _():
        drain(send.at[0:rows, 0:2], send_sem.at[0])
        drain(send.at[0:rows, 2:3], send_sem.at[1])
        drain(conv_in, land_sem.at[0])
        drain(back_in, land_sem.at[1])
        drain(corr_in, land_sem.at[2])

    @pl.when(is_worker)
    def _():
        drain(leave.at[0, 0 : peers - 1], leave_sem.at[0])
        drain(leave.at[1, 0 : peers - 1], leave_sem.at[1])

        @pl.when(foreign)
        def _():
            drain(leave.at[2], leave_sem.at[2])

        @pl.when(jnp.logical_not(foreign))
        def _():
            drain(leave.at[2, 0 : peers - 1], leave_sem.at[2])


def finish(conv_in, back_in, corr_in, direct_signal, direct_gated, cotangent, *rest):
    *results, gating_part, signal_part, filter_part, stage, sem = rest
    parts = (gating_part, signal_part, filter_part)
    lane = 128
    scale = 1.0 / math.sqrt(COARSE * FINE * corr_in.shape[1])

    def gather(values, index, last):
        part = parts[index]
        count = part.shape[0]
        stage[index, 0 : count * 8, :] = values.reshape(count * 8, lane)
        for piece in range(8):
            at = slice(piece * lane, (piece + 1) * lane)
            part[:, at] = last(stage[index, pl.ds(piece, count, stride=8), :], at).astype(part.dtype)
        pltpu.make_async_copy(part, results[index], sem.at[index]).start()

    gather(
        conv_in[...].astype(F32), 0,
        lambda value, at: cotangent[:, at].astype(F32) * (value + direct_signal[:, at]),
    )
    gather(back_in[...].astype(F32), 1, lambda value, at: value + direct_gated[:, at])
    gather(jnp.sum(corr_in[...].astype(F32), axis=1), 2, lambda value, at: value * scale)
    for index in range(3):
        pltpu.make_async_copy(parts[index], results[index], sem.at[index]).wait()


def exchange(signal, gating, cotangent, filters, skip_weight):
    rows, length = signal.shape
    total = COARSE * FINE
    peers = total // length
    operands = (signal, gating, cotangent, filters, skip_weight, *tables(total))
    vmem = pl.BlockSpec(memory_space=pltpu.VMEM)
    hbm = pl.BlockSpec(memory_space=pltpu.HBM)
    return pl.pallas_call(
        kernel,
        out_shape=(
            jax.ShapeDtypeStruct((rows, 8, 128), BF16),
            jax.ShapeDtypeStruct((rows, 8, 128), BF16),
            jax.ShapeDtypeStruct((8, 4, 8, 128), BF16),
            jax.ShapeDtypeStruct((rows, length), F32),
            jax.ShapeDtypeStruct((rows, length), F32),
            jax.ShapeDtypeStruct((rows, length), BF16),
        ),
        in_specs=[hbm] * 9,
        out_specs=(vmem,) * 6,
        scratch_shapes=[
            pltpu.VMEM((rows, length), BF16),
            pltpu.VMEM((rows, length), BF16),
            pltpu.VMEM((rows, length), F32),
            pltpu.VMEM((rows,), F32),
            pltpu.VMEM((rows, 3, 8, 128), BF16),
            pltpu.VMEM((peers, 3, 8, 128), BF16),
            pltpu.VMEM((peers * 8, 128), F32),
            pltpu.VMEM((COARSE, 2 * COARSE), BF16),
            pltpu.VMEM((COARSE, 2 * FINE), F32),
            pltpu.VMEM((2 * FINE, 2 * FINE), BF16),
            pltpu.VMEM((2 * FINE, 2 * FINE), BF16),
            pltpu.VMEM((COARSE, FINE), BF16),
            pltpu.VMEM((3, COARSE, 2 * FINE), F32),
            pltpu.VMEM((2 * COARSE, FINE), BF16),
            pltpu.VMEM((3, peers, 8, 128), BF16),
            pltpu.SemaphoreType.DMA((5,)),
            pltpu.SemaphoreType.DMA((4,)),
            pltpu.SemaphoreType.DMA((4,)),
            pltpu.SemaphoreType.DMA((2,)),
            pltpu.SemaphoreType.DMA((2,)),
            pltpu.SemaphoreType.DMA((3,)),
            pltpu.SemaphoreType.DMA((3,)),
        ],
        compiler_params=pltpu.CompilerParams(
            collective_id=0, has_side_effects=True, vmem_limit_bytes=40 * 1024 * 1024
        ),
        name="exchange",
    )(*[pltpu.with_memory_space_constraint(each, pltpu.HBM) for each in operands])


def per_device(signal, gating, cotangent, filters, skip_weight):
    rows, length = signal.shape
    landed = exchange(signal, gating, cotangent, filters, skip_weight)
    vmem = pl.BlockSpec(memory_space=pltpu.VMEM)
    grad_gating, grad_signal, grad_filters = pl.pallas_call(
        finish,
        out_shape=(
            jax.ShapeDtypeStruct((rows, length), BF16),
            jax.ShapeDtypeStruct((rows, length), BF16),
            jax.ShapeDtypeStruct((8, length), F32),
        ),
        in_specs=[vmem] * 6,
        out_specs=(pl.BlockSpec(memory_space=pl.ANY),) * 3,
        scratch_shapes=[
            pltpu.VMEM((rows, length), BF16),
            pltpu.VMEM((rows, length), BF16),
            pltpu.VMEM((8, length), F32),
            pltpu.VMEM((3, rows * 8, 128), F32),
            pltpu.SemaphoreType.DMA((3,)),
        ],
        compiler_params=pltpu.CompilerParams(vmem_limit_bytes=16 * 1024 * 1024),
        name="finish",
    )(*landed)
    return (grad_signal, grad_gating, grad_filters)


def solution(mesh):
    in_specs = (P("chan", "ctx"), P("chan", "ctx"), P("chan", "ctx"), P(None, "ctx"), P("chan"))
    out_specs = (P("chan", "ctx"), P("chan", "ctx"), P("chan", "ctx"))
    return jax.shard_map(
        per_device, mesh=mesh, in_specs=in_specs, out_specs=out_specs, check_vma=False
    )
```

```python
import math

import jax
import jax.numpy as jnp
import numpy as np
from jax import lax
from jax.experimental import pallas as pl
from jax.experimental.pallas import tpu as pltpu
from jax.sharding import PartitionSpec as P

MESH = pl.DeviceIdType.MESH
F32 = jnp.float32
BF16 = jnp.bfloat16
COARSE = 512
FAR_RING = (4, 3, 5, 2, 6, 1, 7, 0)
FAR_ROW = (2, 1, 3, 0)
FINE = 256
TILE = 256


def tables(total):
    shift = 0.25
    coarse = np.arange(COARSE) - shift
    angle = 2.0 * np.pi * ((coarse[:, None] * coarse[None, :]) / COARSE)
    big = np.concatenate([np.cos(angle), -np.sin(angle)], axis=1)
    fine = np.arange(FINE)
    angle = 2.0 * np.pi * ((coarse[:, None] * fine[None, :]) / total + coarse[:, None] * shift / COARSE)
    turn = np.concatenate([np.cos(angle), -np.sin(angle)], axis=1)
    angle = 2.0 * np.pi * ((fine[:, None] * fine[None, :]) % FINE) / FINE
    cosine, sine = np.cos(angle), np.sin(angle)
    ahead = np.block([[cosine, -sine], [sine, cosine]])
    back = np.block([[cosine, sine], [-sine, cosine]])
    as_bf16 = lambda table: jnp.asarray(table.astype(np.float32)).astype(BF16)
    return (as_bf16(big), jnp.asarray(turn.astype(np.float32)), as_bf16(ahead), as_bf16(back))


def dot(left, right):
    return jnp.dot(left, right, preferred_element_type=F32)


def kernel(
    signal_hbm, gating_hbm, cotangent_hbm, filters_hbm, weight_hbm, big_hbm, turn_hbm, ahead_hbm, back_hbm,
    conv_in, back_in, corr_in, direct_signal, direct_gated, cotangent,
    signal, gating, filters, weight, send, got, stage, big, turn, ahead, back, block, spec, mixed, leave,
    load_sem, table_sem, own_sem, send_sem, got_sem, leave_sem, land_sem,
):
    place = lax.axis_index("ctx")
    chan = lax.axis_index("chan")
    rows = 32
    peers = 128
    lane = 128
    total = COARSE * FINE
    column = place // 4
    row, ring, line = place // 32, column % 8, place % 4
    rows_at = [32 * lax.rem(row + step, 4) for step in range(4)]
    rings_at = [4 * lax.rem(ring + step, 8) for step in range(8)]
    lines_at = [lax.rem(line + step, 4) for step in range(4)]

    def worker_line(parity, channel):
        return 3 * lax.rem(channel, 2) + (1 - 2 * lax.rem(channel, 2)) * (1 - parity)

    own_parity = lax.rem(row + ring, 2)
    workers_at = [worker_line(lax.rem(own_parity + step, 2), chan) for step in range(2)]
    is_worker = line == workers_at[0]
    home = column // 8
    foreign = home != chan

    load_copies = [
        pltpu.make_async_copy(source, target, load_sem.at[index])
        for index, (source, target) in enumerate(
            (
                (signal_hbm, signal),
                (filters_hbm, filters),
                (cotangent_hbm, cotangent),
                (gating_hbm, gating),
                (weight_hbm, weight),
            )
        )
    ]
    for copy in load_copies:
        copy.start()
    table_copies = [
        pltpu.make_async_copy(big_hbm, big, table_sem.at[0]),
        pltpu.make_async_copy(turn_hbm, turn, table_sem.at[1]),
        pltpu.make_async_copy(ahead_hbm, ahead, table_sem.at[2]),
        pltpu.make_async_copy(back_hbm, back, table_sem.at[3]),
    ]

    barrier = pltpu.get_barrier_semaphore()

    def greet(ctx, other):
        pl.semaphore_signal(barrier, inc=1, device_id=(ctx, other), device_id_type=MESH)

    @pl.when(is_worker)
    def _():
        for copy in table_copies:
            copy.start()

        for ring_at in FAR_RING:
            for row_at in FAR_ROW:
                for line_at in range(4):
                    if ring_at or row_at or line_at:
                        greet(rows_at[row_at] + rings_at[ring_at] + lines_at[line_at], chan)

    for hop in range(1, 4):
        other = lax.rem(chan + hop, 4)
        others_at = [worker_line(lax.rem(chan + ring + step, 2), other) for step in range(2)]
        for ring_at in FAR_RING:
            greet(32 * chan + rings_at[ring_at] + others_at[ring_at % 2], other)

    def spread(values, kind):
        for piece in range(8):
            stage[pl.ds(piece, rows, stride=8), :] = values[:, piece * lane : (piece + 1) * lane]
        send[:, kind] = stage[0 : rows * 8, :].reshape(rows, 8, lane).astype(BF16)

    load_copies[0].wait()
    spread(signal[...].astype(F32), 0)
    load_copies[1].wait()
    spread(filters[...], 1)
    load_copies[2].wait()
    load_copies[3].wait()
    gated = (cotangent[...].astype(F32) * gating[...].astype(F32)).astype(BF16)
    spread(gated.astype(F32), 2)
    load_copies[4].wait()
    across = weight[...].reshape(1, rows) * jnp.ones((rows, 1), F32)
    diagonal = lax.broadcasted_iota(jnp.int32, (rows, rows), 0) == lax.broadcasted_iota(
        jnp.int32, (rows, rows), 1
    )
    down = jnp.sum(jnp.where(diagonal, across, 0.0), axis=1, keepdims=True)
    direct_signal[...] = down * signal[...].astype(F32)
    direct_gated[...] = down * gated.astype(F32)

    @pl.when(is_worker)
    def _():
        @pl.when(foreign)
        def _():
            pl.semaphore_wait(barrier, 31 + peers)

        @pl.when(jnp.logical_not(foreign))
        def _():
            pl.semaphore_wait(barrier, 31)

    @pl.when(jnp.logical_not(is_worker))
    def _():
        pl.semaphore_wait(barrier, 32)

    def post(index, low, high, filt, target):
        pltpu.make_async_remote_copy(
            send.at[filt, low:high], got.at[place, low:high], send_sem.at[index], got_sem.at[index],
            device_id=(target, chan), device_id_type=MESH,
        ).start()

    for index, low, high in ((0, 0, 2), (1, 2, 3)):
        for ring_at in FAR_RING:
            for row_at in FAR_ROW:
                base = rows_at[row_at] + rings_at[ring_at]
                filt = base // 4
                target = base + workers_at[(row_at + ring_at) % 2]
                if ring_at or row_at:
                    post(index, low, high, filt, target)
                else:
                    pl.when(jnp.logical_not(is_worker))(lambda: post(index, low, high, filt, target))

    def drain(ref, sem):
        pltpu.make_async_copy(ref, ref, sem).wait()

    def ahead_transform(kind):
        stage[...] = got[:, kind].astype(F32).reshape(peers * 8, lane)
        for half in range(2):
            block[:, half * lane : (half + 1) * lane] = stage[pl.ds(half, COARSE, stride=2), :].astype(BF16)

        for step in range(COARSE // TILE):
            at = pl.ds(step * TILE, TILE)
            real = dot(big[at, 0:COARSE], block[...])
            imag = dot(big[at, COARSE:], block[...])
            cosine = turn[at, 0:FINE]
            sine = turn[at, FINE:]
            turned = jnp.concatenate(
                [real * cosine - imag * sine, real * sine + imag * cosine], axis=1
            ).astype(BF16)
            spec[kind, at, :] = dot(turned, ahead[...])

    def back_transform(left, right, conjugate, kind, after=None):
        for step in range(COARSE // TILE):
            at = pl.ds(step * TILE, TILE)
            left_real = spec[left, at, 0:FINE]
            left_imag = spec[left, at, FINE:]
            right_real = spec[right, at, 0:FINE]
            right_imag = spec[right, at, FINE:]
            if conjugate:
                real = left_real * right_real + left_imag * right_imag
                imag = left_real * right_imag - left_imag * right_real
            else:
                real = left_real * right_real - left_imag * right_imag
                imag = left_real * right_imag + left_imag * right_real
            joined = jnp.concatenate([real, imag], axis=1).astype(BF16)
            half = dot(joined, back[...])
            real, imag = half[:, 0:FINE], half[:, FINE:]
            cosine = turn[at, 0:FINE]
            sine = turn[at, FINE:]
            mixed[at, :] = (real * cosine + imag * sine).astype(BF16)
            low = pl.ds(COARSE + step * TILE, TILE)
            mixed[low, :] = (imag * cosine - real * sine).astype(BF16)

        for step in range(COARSE // TILE):
            at = pl.ds(step * TILE, TILE)
            time = dot(big[at, :], mixed[...]) * (1.0 / total)
            for part in range(2):
                stage[pl.ds(2 * step * TILE + part, TILE, stride=2), :] = time[
                    :, part * lane : (part + 1) * lane
                ]

            if after is not None:
                half = peers * TILE // COARSE
                leave[kind, step * half : (step + 1) * half] = (
                    stage[2 * step * TILE : 2 * (step + 1) * TILE, :].reshape(half, 8, lane).astype(BF16)
                )
                after(step)

        if after is None:
            leave[kind] = stage[...].reshape(peers, 8, lane).astype(BF16)

    def fan(one, with_self):
        for row_at in FAR_ROW:
            for ring_at in FAR_RING:
                for line_at in range(4):
                    target = rows_at[row_at] + rings_at[ring_at] + lines_at[line_at]
                    if ring_at or line_at or row_at:
                        one(target)
                    else:
                        pl.when(with_self)(lambda: one(target))

    def scatter(kind, landing):
        def one(target):
            pltpu.make_async_remote_copy(
                leave.at[kind, target], landing.at[column],
                leave_sem.at[kind], land_sem.at[kind],
                device_id=(target, chan), device_id_type=MESH,
            ).start()

        fan(one, False)
        pltpu.make_async_copy(leave.at[kind, place], landing.at[column], own_sem.at[1 + kind]).start()

    @pl.when(is_worker)
    def _():
        pltpu.make_async_copy(send.at[column], got.at[place], own_sem.at[0]).start()
        for copy in table_copies:
            copy.wait()
        pltpu.make_async_copy(send.at[column], got.at[place], own_sem.at[0]).wait()
        drain(got.at[0 : peers - 1, 0:2], got_sem.at[0])
        ahead_transform(0)
        ahead_transform(1)
        back_transform(0, 1, False, 0)
        scatter(0, conv_in)
        drain(got.at[0 : peers - 1, 2:3], got_sem.at[1])
        ahead_transform(2)
        def halves(one, with_self):
            def send_half(step):
                for ring_at in FAR_RING:
                    for row_at in (2 * step, 2 * step + 1):
                        for line_at in range(4):
                            target = 32 * row_at + rings_at[ring_at] + lines_at[line_at]
                            if ring_at or line_at:
                                one(target)
                            else:
                                pl.when(jnp.logical_or(row != row_at, with_self))(lambda: one(target))

            return send_half

        def send_home(target):
            pltpu.make_async_remote_copy(
                leave.at[2, target], corr_in.at[column % 8, chan],
                leave_sem.at[2], land_sem.at[2],
                device_id=(target, home), device_id_type=MESH,
            ).start()

        back_transform(0, 2, True, 2, halves(send_home, foreign))

        @pl.when(jnp.logical_not(foreign))
        def _():
            pltpu.make_async_copy(leave.at[2, place], corr_in.at[column % 8, chan], own_sem.at[3]).start()

        def send_back(target):
            pltpu.make_async_remote_copy(
                leave.at[1, target], back_in.at[column],
                leave_sem.at[1], land_sem.at[1],
                device_id=(target, chan), device_id_type=MESH,
            ).start()

        back_transform(1, 2, True, 1, halves(send_back, False))
        pltpu.make_async_copy(leave.at[1, place], back_in.at[column], own_sem.at[2]).start()

        drain(send.at[0 : rows - 1, 0:2], send_sem.at[0])
        drain(send.at[0 : rows - 1, 2:3], send_sem.at[1])
        for kind, landing in ((0, conv_in), (1, back_in)):
            pltpu.make_async_copy(leave.at[kind, place], landing.at[column], own_sem.at[1 + kind]).wait()
            drain(landing.at[0 : rows - 1], land_sem.at[kind])

        @pl.when(foreign)
        def _():
            drain(corr_in, land_sem.at[2])

        @pl.when(jnp.logical_not(foreign))
        def _():
            pltpu.make_async_copy(leave.at[2, place], corr_in.at[column % 8, chan], own_sem.at[3]).wait()
            drain(leave.at[2, 0 : rows - 1], land_sem.at[2])

    @pl.when(jnp.logical_not(is_worker))
    def _():
        drain(send.at[0:rows, 0:2], send_sem.at[0])
        drain(send.at[0:rows, 2:3], send_sem.at[1])
        drain(conv_in, land_sem.at[0])
        drain(back_in, land_sem.at[1])
        drain(corr_in, land_sem.at[2])

    @pl.when(is_worker)
    def _():
        drain(leave.at[0, 0 : peers - 1], leave_sem.at[0])
        drain(leave.at[1, 0 : peers - 1], leave_sem.at[1])

        @pl.when(foreign)
        def _():
            drain(leave.at[2], leave_sem.at[2])

        @pl.when(jnp.logical_not(foreign))
        def _():
            drain(leave.at[2, 0 : peers - 1], leave_sem.at[2])


def finish(conv_in, back_in, corr_in, direct_signal, direct_gated, cotangent, *rest):
    *results, gating_part, signal_part, filter_part, stage, sem = rest
    parts = (gating_part, signal_part, filter_part)
    lane = 128
    scale = 1.0 / math.sqrt(COARSE * FINE * corr_in.shape[1])

    def gather(values, index, last):
        part = parts[index]
        count = part.shape[0]
        stage[index, 0 : count * 8, :] = values.reshape(count * 8, lane)
        for piece in range(8):
            at = slice(piece * lane, (piece + 1) * lane)
            part[:, at] = last(stage[index, pl.ds(piece, count, stride=8), :], at).astype(part.dtype)
        pltpu.make_async_copy(part, results[index], sem.at[index]).start()

    gather(
        conv_in[...].astype(F32), 0,
        lambda value, at: cotangent[:, at].astype(F32) * (value + direct_signal[:, at]),
    )
    gather(back_in[...].astype(F32), 1, lambda value, at: value + direct_gated[:, at])
    gather(jnp.sum(corr_in[...].astype(F32), axis=1), 2, lambda value, at: value * scale)
    for index in range(3):
        pltpu.make_async_copy(parts[index], results[index], sem.at[index]).wait()


def exchange(signal, gating, cotangent, filters, skip_weight):
    rows, length = signal.shape
    total = COARSE * FINE
    peers = total // length
    operands = (signal, gating, cotangent, filters, skip_weight, *tables(total))
    vmem = pl.BlockSpec(memory_space=pltpu.VMEM)
    hbm = pl.BlockSpec(memory_space=pltpu.HBM)
    return pl.pallas_call(
        kernel,
        out_shape=(
            jax.ShapeDtypeStruct((rows, 8, 128), BF16),
            jax.ShapeDtypeStruct((rows, 8, 128), BF16),
            jax.ShapeDtypeStruct((8, 4, 8, 128), BF16),
            jax.ShapeDtypeStruct((rows, length), F32),
            jax.ShapeDtypeStruct((rows, length), F32),
            jax.ShapeDtypeStruct((rows, length), BF16),
        ),
        in_specs=[hbm] * 9,
        out_specs=(vmem,) * 6,
        scratch_shapes=[
            pltpu.VMEM((rows, length), BF16),
            pltpu.VMEM((rows, length), BF16),
            pltpu.VMEM((rows, length), F32),
            pltpu.VMEM((rows,), F32),
            pltpu.VMEM((rows, 3, 8, 128), BF16),
            pltpu.VMEM((peers, 3, 8, 128), BF16),
            pltpu.VMEM((peers * 8, 128), F32),
            pltpu.VMEM((COARSE, 2 * COARSE), BF16),
            pltpu.VMEM((COARSE, 2 * FINE), F32),
            pltpu.VMEM((2 * FINE, 2 * FINE), BF16),
            pltpu.VMEM((2 * FINE, 2 * FINE), BF16),
            pltpu.VMEM((COARSE, FINE), BF16),
            pltpu.VMEM((3, COARSE, 2 * FINE), F32),
            pltpu.VMEM((2 * COARSE, FINE), BF16),
            pltpu.VMEM((3, peers, 8, 128), BF16),
            pltpu.SemaphoreType.DMA((5,)),
            pltpu.SemaphoreType.DMA((4,)),
            pltpu.SemaphoreType.DMA((4,)),
            pltpu.SemaphoreType.DMA((2,)),
            pltpu.SemaphoreType.DMA((2,)),
            pltpu.SemaphoreType.DMA((3,)),
            pltpu.SemaphoreType.DMA((3,)),
        ],
        compiler_params=pltpu.CompilerParams(
            collective_id=0, has_side_effects=True, vmem_limit_bytes=40 * 1024 * 1024
        ),
        name="exchange",
    )(*[pltpu.with_memory_space_constraint(each, pltpu.HBM) for each in operands])


def per_device(signal, gating, cotangent, filters, skip_weight):
    rows, length = signal.shape
    landed = exchange(signal, gating, cotangent, filters, skip_weight)
    vmem = pl.BlockSpec(memory_space=pltpu.VMEM)
    grad_gating, grad_signal, grad_filters = pl.pallas_call(
        finish,
        out_shape=(
            jax.ShapeDtypeStruct((rows, length), BF16),
            jax.ShapeDtypeStruct((rows, length), BF16),
            jax.ShapeDtypeStruct((8, length), F32),
        ),
        in_specs=[vmem] * 6,
        out_specs=(pl.BlockSpec(memory_space=pl.ANY),) * 3,
        scratch_shapes=[
            pltpu.VMEM((rows, length), BF16),
            pltpu.VMEM((rows, length), BF16),
            pltpu.VMEM((8, length), F32),
            pltpu.VMEM((3, rows * 8, 128), F32),
            pltpu.SemaphoreType.DMA((3,)),
        ],
        compiler_params=pltpu.CompilerParams(vmem_limit_bytes=16 * 1024 * 1024),
        name="finish",
    )(*landed)
    return (grad_signal, grad_gating, grad_filters)


def solution(mesh):
    in_specs = (P("chan", "ctx"), P("chan", "ctx"), P("chan", "ctx"), P(None, "ctx"), P("chan"))
    out_specs = (P("chan", "ctx"), P("chan", "ctx"), P("chan", "ctx"))
    return jax.shard_map(
        per_device, mesh=mesh, in_specs=in_specs, out_specs=out_specs, check_vma=False
    )
```
